128 devices in a mesh: seq: 16 (over x_lo, y, core), head: 8 (over x_hi, z).
Axes of the slice: x: 4 (x_hi: 2, x_lo: 2; x = x_hi * 2 + x_lo), y: 4, z: 4, core: 2. Of those that a mesh axis runs over, the one named last changes fastest.
Arguments:
- queries: bfloat16 [6144, 4096], P('seq', 'head'), may hold values from -108 to 108
- keys_in: bfloat16 [6144, 4096], P('seq', 'head'), may hold values from -4 to 4
- values: bfloat16 [6144, 4096], P('seq', 'head'), may hold values from -6 to 6
- out_grad: bfloat16 [6144, 4096], P('seq', 'head'), may hold values from -6 to 6
- out_weight: bfloat16 [4096, 4096], P('head'), may hold values from -0.09375 to 0.09375
- doc_ids: int32 [6144], P('seq'), may hold values from 0 to 7, never falling along the last dimension, each value on 1 to 3456 neighbouring positions
Outputs:
- query_grad: bfloat16 [6144, 4096], P('seq', 'head')
- key_grad: bfloat16 [6144, 4096], P('seq', 'head')
- value_grad: bfloat16 [6144, 4096], P('seq', 'head')
The draws below stay inside these ranges and needn't reach their ends.
Inputs may be any that keep to these rules, and one draw needn't show every extreme that they name: `doc_ids`: document ids never fall along the rows.
All inputs are finite; a program needn't handle non-finite values.
Results may differ from the reference program's by a relative error of at most 0.0085.
Values may be sent and summed in bfloat16 or wider, within the bound.
A program may use at most 192 MiB of HBM per device.

```python
import math
import jax
import jax.numpy as jnp
import numpy as np
from jax import lax

D = 4096
HEADS = 32
HD = 128
S_DEV = 384
TOKENS = 6144


def shared_keys(key):
    return jnp.clip(jax.random.normal(jax.random.fold_in(key, 11), (TOKENS, HEADS * HD), jnp.float32), -4.0, 4.0)


def draw_keys_in(key, part):
    base_keys = shared_keys(key)
    return base_keys.astype(jnp.bfloat16)


def draw_queries(key, part):
    drawn = jnp.clip(jax.random.normal(jax.random.fold_in(key, 13), (TOKENS, HEADS * HD), jnp.float32), -4.0, 4.0)
    return drawn.astype(jnp.bfloat16)


def block_levels(stream_key, dims, split, smallest, largest):
    gain, own = 1.0, jax.random.fold_in(stream_key, 6)
    for position, shards_of in split:
        draws = jnp.exp(jax.random.uniform(jax.random.fold_in(own, position), (shards_of,), jnp.float32, smallest / len(split), largest / len(split)))
        gain = gain * jnp.repeat(draws, dims[position] // shards_of).reshape([-1 if axis == position else 1 for axis in range(len(dims))])
    return gain


def split_up(amount, total, most, lean):
    loads = [(1 << 20) // math.isqrt(grade ** lean) + 1 for grade in range(2, amount + 1)]
    spare, given = total - most - (amount - 1), [1] * (amount - 1)
    while spare > 0:
        free = [i for i in range(amount - 1) if given[i] < most]
        whole, remaining = sum([loads[i] for i in free]), spare
        for i in free:
            extra = min(most - given[i], max(1, remaining * loads[i] // whole), spare)
            given[i] = given[i] + extra
            spare = spare - extra
    return np.array([most] + given)


def uneven_parts(stream_key, count, total, most, skew):
    if count == 2:
        one = jax.random.randint(stream_key, (), max(1, total - most), min(most, total - 1) + 1)
        return jnp.stack([one, total - one])
    tallies = jnp.asarray(split_up(count, total, most, skew), jnp.int32)
    twos = (count - 1) // 2
    donor, taker = tallies[1:1 + 2 * twos:2], tallies[2:2 + 2 * twos:2]
    slack = jnp.minimum(donor - 1, most - taker)
    shifted = jax.random.randint(jax.random.fold_in(stream_key, 1), (twos,), 0, 1 << 20) % (slack + 1)
    tallies = tallies.at[1:1 + 2 * twos:2].set(donor - shifted).at[2:2 + 2 * twos:2].set(taker + shifted)
    return tallies[jax.random.permutation(jax.random.fold_in(stream_key, 2), count)]


def bell_draw(stream_key, shape, spread, limit, shards=(), held_as=jnp.bfloat16):
    result = spread * jax.random.normal(stream_key, shape, jnp.float32)
    if shards:
        result = result * block_levels(stream_key, shape, shards, -0.22, 0.18)
    return jnp.clip(result, -limit, limit).astype(held_as)


def setup_inputs(seed: int = 0) -> dict:
    key_list = jax.random.split(jax.random.key(seed), 7)
    return {
        "queries": draw_queries(jax.random.fold_in(key_list[6], 71), 0),
        "keys_in": draw_keys_in(jax.random.fold_in(key_list[6], 71), 0),
        "values": bell_draw(key_list[2], (TOKENS, HEADS * HD), 1.0, 6.0, ((0, 16), (1, 8))),
        "out_grad": bell_draw(key_list[3], (TOKENS, D), 1.0, 6.0, ((0, 16), (1, 8))),
        "out_weight": bell_draw(key_list[4], (HEADS * HD, D), D ** -0.5, 0.09375, ((0, 8),)),
        "doc_ids": jnp.searchsorted(jnp.cumsum(uneven_parts(key_list[5], 8, TOKENS, TOKENS // 2 + S_DEV, 2)), jnp.arange(TOKENS), side="right").astype(jnp.int32),
    }


def reference(queries, keys_in, values, out_grad, out_weight, doc_ids):
    grad_attn = jnp.dot(out_grad, out_weight.T, preferred_element_type=jnp.float32).astype(jnp.bfloat16)
    scale = HD ** -0.5
    positions = jnp.arange(TOKENS, dtype=jnp.int32)
    allowed = (positions[None, :] <= positions[:, None]) & (doc_ids[None, :] == doc_ids[:, None])

    def one_head(head_index):
        offset = (head_index * HD).astype(jnp.int32)
        query_h = lax.dynamic_slice_in_dim(queries, offset, HD, 1)
        key_h = lax.dynamic_slice_in_dim(keys_in, offset, HD, 1)
        value_h = lax.dynamic_slice_in_dim(values, offset, HD, 1)
        grad_h = lax.dynamic_slice_in_dim(grad_attn, offset, HD, 1)
        scores = jnp.dot(query_h, key_h.T, preferred_element_type=jnp.float32) * scale
        masked = jnp.where(allowed, scores, -1e30)
        row_max = jnp.max(masked, axis=1)
        row_total = jnp.sum(jnp.where(allowed, jnp.exp(masked - row_max[:, None]), 0.0), axis=1)
        log_total = row_max + jnp.log(row_total)
        probs = jnp.where(allowed, jnp.exp(masked - log_total[:, None]), 0.0)
        grad_probs = jnp.dot(grad_h, value_h.T, preferred_element_type=jnp.float32)
        row_dot = jnp.sum(probs * grad_probs, axis=1)
        grad_scores = (probs * (grad_probs - row_dot[:, None])).astype(jnp.bfloat16)
        query_grad = (scale * jnp.dot(grad_scores, key_h, preferred_element_type=jnp.float32)).astype(jnp.bfloat16)
        key_grad = (scale * jnp.dot(grad_scores.T, query_h, preferred_element_type=jnp.float32)).astype(jnp.bfloat16)
        value_grad = jnp.dot(probs.astype(jnp.bfloat16).T, grad_h, preferred_element_type=jnp.float32).astype(jnp.bfloat16)
        return query_grad, key_grad, value_grad

    query_all, key_all, value_all = lax.map(one_head, jnp.arange(HEADS, dtype=jnp.int32))

    def flatten(stacked):
        return jnp.transpose(stacked, (1, 0, 2)).reshape(TOKENS, HEADS * HD)

    return flatten(query_all), flatten(key_all), flatten(value_all)
```

```python
import functools

import jax
import jax.numpy as jnp
from jax import lax
from jax.experimental import pallas as pl
from jax.experimental.pallas import tpu as pltpu
from jax.sharding import PartitionSpec as P

HD = 128
ROWS = 384
COLS = 512
HEADS_LOCAL = 4
TOTAL = 6144
HALF = 3072
QT = 256
KT = 256
QLOCAL = 1536
NCH = 4
CH = ROWS // NCH
NEG = -1e30
SCALE = HD ** -0.5
LOG2E = 1.4426950408889634
MESH = pl.DeviceIdType.MESH
NT = (((1,), (1,)), ((), ()))
TN = (((0,), (0,)), ((), ()))
NN = (((1,), (0,)), ((), ()))


def place():
    s = lax.axis_index("seq")
    g = lax.axis_index("head")
    x = s // 8
    y = (s // 2) % 4
    k = s % 2
    return s, g, x, y, k


def seq_of(x, y, k):
    return (x * 4 + y) * 2 + k


def remote(src, dst, send, recv, seq, head):
    return pltpu.make_async_remote_copy(
        src_ref=src,
        dst_ref=dst,
        send_sem=send,
        recv_sem=recv,
        device_id={"seq": seq, "head": head},
        device_id_type=MESH,
    )


def barrier_with(peers):
    barrier = pltpu.get_barrier_semaphore()
    for seq, head in peers:
        pl.semaphore_signal(
            barrier, inc=1, device_id={"seq": seq, "head": head}, device_id_type=MESH
        )
    pl.semaphore_wait(barrier, len(peers))


def block_rows(s):
    return pl.ds(pl.multiple_of(s * ROWS, 128), ROWS)


def head_cols(y):
    return pl.ds(pl.multiple_of(y * HD, HD), HD)


def slot_of(y, k, j):
    u = 3 * k + j
    return (y + u // 2) % 2, ((3 * y + u // 2) // 2) * 2 + u % 2


def gather_kernel(
    q_ref, k_ref, v_ref, og_ref, w_hbm, doc_ref,
    ko, vo, qo, do, doco,
    land, w_ref, acc, grad,
    g_send, g_recv, y_send, y_recv, sib_send, sib_recv, x_send, x_recv,
    q_send, q_recv, o_send, o_recv, d_send, d_recv, w_sem, l_sem,
):
    s, g, x, y, k = place()
    xh, z = g // 4, g % 4
    up = xh * 4 + (z + 1) % 4
    down = xh * 4 + (z + 3) % 4
    across = (1 - xh) * 4 + z
    sibling = seq_of(x, y, 1 - k)
    other = seq_of(1 - x, y, k)

    barrier_with(
        [((s + i) % 16, g) for i in range(1, 16)] + [(s, up), (s, down), (s, across)]
    )
    w_copy = pltpu.make_async_copy(w_hbm, w_ref, w_sem)
    w_copy.start()

    sends = []

    def go(copy):
        copy.start()
        sends.append(copy)

    def rows(c):
        return pl.ds(c * CH, CH)

    order = [(0, 2), (1, 3), (2, 0), (3, 1)]

    def ring(n, src, slot, c, head):
        return remote(src, land.at[slot, rows(c)], g_send.at[n, c], g_recv.at[slot, c], s, head)

    for up_c, down_c in order:
        go(ring(0, og_ref.at[rows(up_c)], 1, up_c, up))
        go(ring(1, og_ref.at[rows(down_c)], 2, down_c, down))
        go(ring(2, og_ref.at[rows(up_c)], 4, up_c, across))

    mine = block_rows(s)
    local = []
    for i, (src, dst) in enumerate(((k_ref, ko), (v_ref, vo))):
        copy = pltpu.make_async_copy(src.at[:, head_cols(y)], dst.at[mine], l_sem.at[i])
        copy.start()
        local.append(copy)
    for dy in (2, 1, 3):
        ty = (y + dy) % 4
        for i, (src, dst) in enumerate(((k_ref, ko), (v_ref, vo))):
            go(remote(src.at[:, head_cols(ty)], dst.at[mine], y_send.at[dy, i],
                      y_recv.at[dy, i], seq_of(x, ty, k), g))

    def x_copy(src, dst, where, dy, i):
        return remote(src, dst.at[where], x_send.at[dy, i], x_recv.at[dy, i], other, g)

    def sib_copy(src, dst, where, n, i):
        return remote(src, dst.at[where], sib_send.at[n, i], sib_recv.at[n, i], sibling, g)

    for i, (src, dst) in enumerate(((k_ref, ko), (v_ref, vo))):
        go(sib_copy(src.at[:, head_cols(y)], dst, mine, 0, i))

    @pl.when(x == 0)
    def _():
        for i, (src, dst) in enumerate(((k_ref, ko), (v_ref, vo))):
            x_copy(src.at[:, head_cols(y)], dst, mine, 0, i).start()

    def spread(src, dst, send, recv):
        for dy in (2, 1, 3, 0):
            ty = (y + dy) % 4
            for j in range(3):
                core, slot = slot_of(y, k, j)
                piece = src.at[pl.ds(j * HD, HD), head_cols(ty)]
                there = dst.at[pl.ds(pl.multiple_of(slot * HD, HD), HD)]
                if dy:
                    go(remote(piece, there, send.at[dy, j], recv.at[slot], seq_of(x, ty, core), g))
                else:
                    @pl.when(core != k)
                    def _():
                        remote(piece, there, send.at[0, j], recv.at[slot], sibling, g).start()

                    @pl.when(core == k)
                    def _():
                        pltpu.make_async_copy(piece, there, recv.at[slot]).start()

    def drain(src, dst, send, recv):
        for j in range(3):
            core, slot = slot_of(y, k, j)
            piece = src.at[pl.ds(j * HD, HD), head_cols(y)]
            there = dst.at[pl.ds(pl.multiple_of(slot * HD, HD), HD)]

            @pl.when(core != k)
            def _():
                remote(piece, there, send.at[0, j], recv.at[slot], sibling, g).wait_send()
        for slot in range(12):
            there = dst.at[pl.ds(slot * HD, HD)]
            pltpu.make_async_copy(there, there, recv.at[slot]).wait()

    spread(q_ref, qo, q_send, q_recv)
    for i in range(1, 16):
        go(remote(doc_ref, doco.at[s], d_send.at[i], d_recv.at[i], (s + i) % 16, g))
    own_doc = pltpu.make_async_copy(doc_ref, doco.at[s], d_recv.at[0])
    own_doc.start()

    def got(slot, c):
        ring(0, land.at[slot, rows(c)], slot, c, up).wait_recv()

    def relay_kv(dy):
        where = block_rows(seq_of(x, (y + 4 - dy) % 4, k))
        for i, dst in enumerate((ko, vo)):
            remote(dst.at[where], dst.at[where], y_send.at[dy, i], y_recv.at[dy, i], sibling, g).wait_recv()

            @pl.when(x == 0)
            def _():
                x_copy(dst.at[where], dst, where, dy, i).start()
            go(sib_copy(dst.at[where], dst, where, dy, i))

    def from_x(dy):
        where = block_rows(seq_of(0, (y + 4 - dy) % 4, k))

        @pl.when(x == 1)
        def _():
            for i, dst in enumerate((ko, vo)):
                x_copy(dst.at[where], dst, where, dy, i).wait_recv()
                sib_copy(dst.at[where], dst, where, 4 + dy, i).start()

    for c in (0, 1):
        got(1, c)
        go(ring(3, land.at[1, rows(c)], 3, c, up))
        got(2, c + 2)
        go(ring(3, land.at[2, rows(c + 2)], 3, c + 2, down))
    relay_kv(1)
    relay_kv(3)
    for c in (0, 1):
        got(4, c)
        go(ring(4, land.at[4, rows(c)], 5, c, up))
        go(ring(5, land.at[4, rows(c)], 6, c, down))
    relay_kv(2)
    for c in (2, 3):
        got(4, c)
        go(ring(4, land.at[4, rows(c)], 5, c, up))
        go(ring(5, land.at[4, rows(c)], 6, c, down))
    from_x(0)

    w_copy.wait()

    def product(slot, head):
        block = og_ref[...] if slot == 0 else land[slot]
        weights = w_ref[:, pl.ds(pl.multiple_of(head * COLS, COLS), COLS)]
        part = lax.dot_general(block, weights, NT, preferred_element_type=jnp.float32)
        acc[...] = part if slot == 0 else acc[...] + part

    far = xh * 4 + (z + 2) % 4
    product(0, g)
    for c in (2, 3):
        got(1, c)
        got(2, c - 2)
    product(1, down)
    product(2, up)
    for c in range(4):
        got(3, c)
    product(3, far)
    product(4, across)
    from_x(1)
    for c in (0, 1):
        got(5, c)
        go(ring(6, land.at[5, rows(c)], 7, c, up))
    from_x(3)
    for c in (2, 3):
        got(6, c)
        go(ring(6, land.at[6, rows(c)], 7, c, down))
    from_x(2)
    turn = (1 - xh) * 4
    for c in (2, 3):
        got(5, c)
    product(5, turn + (z + 3) % 4)
    for c in (0, 1):
        got(6, c)
    product(6, turn + (z + 1) % 4)
    for c in range(4):
        got(7, c)
    product(7, turn + (z + 2) % 4)
    grad[...] = acc[...].astype(jnp.bfloat16)
    spread(grad, do, o_send, o_recv)

    for copy in local:
        copy.wait()
    own_doc.wait()
    for i in range(1, 16):
        remote(doc_ref, doco.at[(s + 16 - i) % 16], d_send.at[i], d_recv.at[i], s, g).wait_recv()
    for dy in range(4):
        where = block_rows(seq_of(x, (y + 4 - dy) % 4, 1 - k))
        for i, dst in enumerate((ko, vo)):
            sib_copy(dst.at[where], dst, where, dy, i).wait_recv()

    @pl.when(x == 0)
    def _():
        for dy in range(4):
            where = block_rows(seq_of(x, (y + 4 - dy) % 4, k))
            for i, dst in enumerate((ko, vo)):
                x_copy(dst.at[where], dst, where, dy, i).wait_send()

    @pl.when(x == 1)
    def _():
        for dy in range(4):
            where = block_rows(seq_of(0, (y + 4 - dy) % 4, 1 - k))
            for i, dst in enumerate((ko, vo)):
                copy = sib_copy(dst.at[where], dst, where, 4 + dy, i)
                copy.wait_recv()
                copy.wait_send()
    drain(q_ref, qo, q_send, q_recv)
    drain(grad, do, o_send, o_recv)
    for copy in sends:
        copy.wait_send()


def gather_call(queries, keys_in, values, out_grad, out_weight, docs):
    vm = pl.BlockSpec(memory_space=pltpu.VMEM)
    anyspace = pl.BlockSpec(memory_space=pl.ANY)
    dma = pltpu.SemaphoreType.DMA
    bf = jnp.bfloat16
    return pl.pallas_call(
        gather_kernel,
        out_shape=(
            jax.ShapeDtypeStruct((TOTAL, HD), bf),
            jax.ShapeDtypeStruct((TOTAL, HD), bf),
            jax.ShapeDtypeStruct((QLOCAL, HD), bf),
            jax.ShapeDtypeStruct((QLOCAL, HD), bf),
            jax.ShapeDtypeStruct((16, 3, HD), jnp.int32),
        ),
        in_specs=[vm, vm, vm, vm, anyspace, vm],
        out_specs=(anyspace,) * 5,
        scratch_shapes=[
            pltpu.VMEM((8, ROWS, COLS), bf),
            pltpu.VMEM((COLS, 4096), bf),
            pltpu.VMEM((ROWS, COLS), jnp.float32),
            pltpu.VMEM((ROWS, COLS), bf),
            dma((7, NCH)), dma((8, NCH)), dma((4, 2)), dma((4, 2)),
            dma((8, 2)), dma((8, 2)), dma((4, 2)), dma((4, 2)),
            dma((4, 3)), dma((12,)), dma((4, 3)), dma((12,)),
            dma((16,)), dma((16,)), dma, dma((2,)),
        ],
        compiler_params=pltpu.CompilerParams(
            collective_id=0, has_side_effects=True, vmem_limit_bytes=48 << 20
        ),
        name="spread_rows",
    )(queries, keys_in, values, out_grad, out_weight, docs)


def attention_kernel(
    doc_s, doc_v, q_ref, o_ref, k_ref, v_ref,
    dq_ref, dk_ref, dv_ref,
    p_buf, g_buf, m_buf, dk_acc, dv_acc, dq_acc, first,
):
    s, g, x, y, k = place()
    docs = doc_v[...]
    first[0] = 0
    starts = [jnp.int32(0)]
    for d in range(1, 8):
        count = jnp.sum(jnp.where(docs < d, 1, 0))
        first[d] = count
        starts.append(count)
    dk_acc[...] = jnp.zeros_like(dk_acc)
    dv_acc[...] = jnp.zeros_like(dv_acc)
    factor = SCALE * LOG2E
    lane = lax.broadcasted_iota(jnp.int32, (1, QT), 1)
    sub = lax.broadcasted_iota(jnp.int32, (KT, QT), 0)

    @pl.loop(0, QLOCAL // QT)
    def _(t):
        q0 = pl.multiple_of(HALF * x + QT * (2 * t + k), QT)
        mine = pl.ds(pl.multiple_of(t * QT, QT), QT)
        q_tile = q_ref[mine, :]
        o_tile = o_ref[mine, :]
        low = first[doc_s[q0 // ROWS, q0 % ROWS]]
        k_low = low // KT
        k_end = q0 // KT + 1
        row = q0 // HD
        doc_q = jnp.concatenate([doc_v[pl.ds(row, 1), :], doc_v[pl.ds(row + 1, 1), :]], axis=1)
        start = jnp.zeros((1, QT), jnp.int32)
        for d in range(1, 8):
            start = jnp.where(doc_q == d, starts[d], start)
        pos = q0 + lane

        def forward(kt, carry):
            m, total, weighted = carry
            keys = pl.ds(pl.multiple_of(kt * KT, KT), KT)
            scores = lax.dot_general(k_ref[keys, :], q_tile, NT, preferred_element_type=jnp.float32)
            key = kt * KT + sub
            scores = jnp.where((key >= start) & (key <= pos), scores, NEG)
            m_new = jnp.maximum(m, jnp.max(scores, axis=0, keepdims=True))
            p = jnp.exp2((scores - m_new) * factor)
            gp = lax.dot_general(v_ref[keys, :], o_tile, NT, preferred_element_type=jnp.float32)
            p_buf[kt] = p
            g_buf[kt] = gp
            m_buf[kt] = m_new
            fix = jnp.exp2((m - m_new) * factor)
            return (
                m_new,
                total * fix + jnp.sum(p, axis=0, keepdims=True),
                weighted * fix + jnp.sum(p * gp, axis=0, keepdims=True),
            )

        zero = jnp.zeros((1, QT), jnp.float32)
        m, total, weighted = lax.fori_loop(
            k_low, k_end, forward, (jnp.full((1, QT), NEG, jnp.float32), zero, zero)
        )
        inverse = 1.0 / total
        dot_row = weighted * inverse
        dq_acc[...] = jnp.zeros_like(dq_acc)

        @pl.loop(k_low, k_end)
        def _(kt):
            keys = pl.ds(pl.multiple_of(kt * KT, KT), KT)
            probs = p_buf[kt] * (jnp.exp2((m_buf[kt] - m) * factor) * inverse)
            ds = (probs * (g_buf[kt] - dot_row)).astype(jnp.bfloat16)
            dv_acc[keys, :] += lax.dot_general(
                probs.astype(jnp.bfloat16), o_tile, NN, preferred_element_type=jnp.float32
            )
            dk_acc[keys, :] += lax.dot_general(ds, q_tile, NN, preferred_element_type=jnp.float32)
            dq_acc[...] += lax.dot_general(
                ds, k_ref[keys, :], TN, preferred_element_type=jnp.float32
            )

        dq_ref[mine, :] = (dq_acc[...] * SCALE).astype(jnp.bfloat16)

    dk_ref[...] = (dk_acc[...] * SCALE).astype(jnp.bfloat16)
    dv_ref[...] = dv_acc[...].astype(jnp.bfloat16)


def attention_call(docs, q, o, k, v):
    vm = pl.BlockSpec(memory_space=pltpu.VMEM)
    sm = pl.BlockSpec(memory_space=pltpu.SMEM)
    bf, f32 = jnp.bfloat16, jnp.float32
    tiles = TOTAL // KT
    return pl.pallas_call(
        attention_kernel,
        out_shape=(
            jax.ShapeDtypeStruct((QLOCAL, HD), bf),
            jax.ShapeDtypeStruct((TOTAL, HD), bf),
            jax.ShapeDtypeStruct((TOTAL, HD), bf),
        ),
        in_specs=[sm, vm, vm, vm, vm, vm],
        out_specs=(vm, vm, vm),
        scratch_shapes=[
            pltpu.VMEM((tiles, KT, QT), f32),
            pltpu.VMEM((tiles, KT, QT), f32),
            pltpu.VMEM((tiles, 1, QT), f32),
            pltpu.VMEM((TOTAL, HD), f32),
            pltpu.VMEM((TOTAL, HD), f32),
            pltpu.VMEM((QT, HD), f32),
            pltpu.SMEM((8,), jnp.int32),
        ],
        compiler_params=pltpu.CompilerParams(vmem_limit_bytes=60 << 20),
        name="attention_grads",
    )(docs.reshape(16, ROWS), docs.reshape(48, HD), q, o, k, v)


def return_kernel(
    dq_ref, dk_ref, dv_ref,
    qo, ko, vo,
    sib_buf, x_buf, stage,
    q_send, q_recv, sib_send, sib_recv, x_send, x_recv, y_send, y_recv,
):
    s, g, x, y, k = place()
    sibling = seq_of(x, y, 1 - k)
    other = seq_of(1 - x, y, k)
    peers = [(sibling, g), (other, g)]
    for dy in (1, 2, 3):
        for dk in (0, 1):
            peers.append((seq_of(x, (y + dy) % 4, (k + dk) % 2), g))
    barrier_with(peers)
    parts = (dk_ref, dv_ref)
    outs = (ko, vo)
    order = (2, 1, 3, 0)

    def sib_copy(col, dy, i):
        src = parts[i].at[block_rows(seq_of(col, (y + dy) % 4, 1 - k))]
        n = col * 4 + dy
        return remote(src, sib_buf.at[n, i], sib_send.at[n, i], sib_recv.at[n, i], sibling, g)

    def x_copy(dy, i):
        return remote(stage.at[dy, i], x_buf.at[dy, i], x_send.at[dy, i], x_recv.at[dy, i], other, g)

    def y_copy(n, dy, i):
        return remote(
            stage.at[n, i], outs[i].at[:, head_cols(y)], y_send.at[dy, i], y_recv.at[dy, i],
            seq_of(x, (y + dy) % 4, k), g,
        )

    def y_local(n, i):
        return pltpu.make_async_copy(stage.at[n, i], outs[i].at[:, head_cols(y)], y_recv.at[0, i])

    for dy in order:
        for i in range(2):
            sib_copy(0, dy, i).start()

    @pl.when(x == 1)
    def _():
        for dy in order:
            for i in range(2):
                sib_copy(1, dy, i).start()

    def q_piece(n):
        unit = (2 * (n // 2) + k) * 2 + n % 2
        ty, u = unit // 6, unit % 6
        tk, j = u // 3, u % 3
        src = dq_ref.at[pl.ds(n * HD, HD)]
        dst = qo.at[pl.ds(pl.multiple_of(j * HD, HD), HD), head_cols(y)]
        return ty, tk, j, src, dst

    for n in range(12):
        ty, tk, j, src, dst = q_piece(n)
        here = (ty == y) & (tk == k)
        sem = q_recv.at[y, j]

        @pl.when(here)
        def _():
            pltpu.make_async_copy(src, dst, sem).start()

        @pl.when(jnp.logical_not(here))
        def _():
            remote(src, dst, q_send.at[n], sem, seq_of(x, ty, tk), g).start()

    def summed(col, dy, i, extra):
        sib_copy(col, dy, i).wait_recv()
        rows = block_rows(seq_of(col, (y + dy) % 4, k))
        total = parts[i][rows, :].astype(jnp.float32) + sib_buf[col * 4 + dy, i].astype(jnp.float32)
        if extra:
            x_copy(dy, i).wait_recv()
            total = total + x_buf[dy, i].astype(jnp.float32)
        return total.astype(jnp.bfloat16)

    @pl.when(x == 1)
    def _():
        for dy in order:
            for i in range(2):
                stage[dy, i] = summed(0, dy, i, False)
                x_copy(dy, i).start()
        for dy in order:
            for i in range(2):
                stage[4 + dy, i] = summed(1, dy, i, False)
                if dy:
                    y_copy(4 + dy, dy, i).start()
                else:
                    y_local(4, i).start()

    @pl.when(x == 0)
    def _():
        for dy in order:
            for i in range(2):
                stage[dy, i] = summed(0, dy, i, True)
                if dy:
                    y_copy(dy, dy, i).start()
                else:
                    y_local(0, i).start()

    for ty in range(4):
        for j in range(3):
            dst = qo.at[pl.ds(j * HD, HD), pl.ds(ty * HD, HD)]
            pltpu.make_async_copy(dst, dst, q_recv.at[ty, j]).wait()
    for n in range(12):
        ty, tk, j, src, dst = q_piece(n)

        @pl.when(jnp.logical_not((ty == y) & (tk == k)))
        def _():
            remote(src, dst, q_send.at[n], q_recv.at[y, j], seq_of(x, ty, tk), g).wait_send()
    for dy in range(4):
        for i in range(2):
            dst = outs[i].at[:, head_cols((y + 4 - dy) % 4)]
            pltpu.make_async_copy(dst, dst, y_recv.at[dy, i]).wait()
            sib_copy(0, dy, i).wait_send()
            if dy:
                y_copy(dy, dy, i).wait_send()

    @pl.when(x == 1)
    def _():
        for dy in range(4):
            for i in range(2):
                sib_copy(1, dy, i).wait_send()
                x_copy(dy, i).wait_send()


def return_call(dq, dk, dv):
    vm = pl.BlockSpec(memory_space=pltpu.VMEM)
    anyspace = pl.BlockSpec(memory_space=pl.ANY)
    dma = pltpu.SemaphoreType.DMA
    bf = jnp.bfloat16
    return pl.pallas_call(
        return_kernel,
        out_shape=(jax.ShapeDtypeStruct((ROWS, COLS), bf),) * 3,
        in_specs=[vm, vm, vm],
        out_specs=(anyspace,) * 3,
        scratch_shapes=[
            pltpu.VMEM((8, 2, ROWS, HD), bf),
            pltpu.VMEM((4, 2, ROWS, HD), bf),
            pltpu.VMEM((8, 2, ROWS, HD), bf),
            dma((12,)), dma((4, 3)), dma((8, 2)), dma((8, 2)),
            dma((4, 2)), dma((4, 2)), dma((4, 2)), dma((4, 2)),
        ],
        compiler_params=pltpu.CompilerParams(
            collective_id=1, has_side_effects=True, vmem_limit_bytes=40 << 20
        ),
        name="return_grads",
    )(dq, dk, dv)


def per_device(queries, keys_in, values, out_grad, out_weight, doc_ids):
    k, v, q, o, docs = gather_call(
        queries, keys_in, values, out_grad, out_weight, doc_ids.reshape(3, HD)
    )
    dq, dk, dv = attention_call(docs, q, o, k, v)
    return return_call(dq, dk, dv)


def solution(mesh):
    in_specs = (
        P("seq", "head"),
        P("seq", "head"),
        P("seq", "head"),
        P("seq", "head"),
        P("head", None),
        P("seq"),
    )
    out_specs = (P("seq", "head"), P("seq", "head"), P("seq", "head"))
    return jax.shard_map(
        per_device, mesh=mesh, in_specs=in_specs, out_specs=out_specs, check_vma=False
    )
```

```python
import functools

import jax
import jax.numpy as jnp
from jax import lax
from jax.experimental import pallas as pl
from jax.experimental.pallas import tpu as pltpu
from jax.sharding import PartitionSpec as P

HD = 128
ROWS = 384
COLS = 512
HEADS_LOCAL = 4
TOTAL = 6144
QT = 256
KT = 512
QLOCAL = 1536
NCH = 4
CH = ROWS // NCH
NEG = -1e30
SCALE = HD ** -0.5
LOG2E = 1.4426950408889634
MESH = pl.DeviceIdType.MESH
NT = (((1,), (1,)), ((), ()))
TN = (((0,), (0,)), ((), ()))
NN = (((1,), (0,)), ((), ()))


def place():
    s = lax.axis_index("seq")
    g = lax.axis_index("head")
    x = s // 8
    y = (s // 2) % 4
    k = s % 2
    return s, g, x, y, k


def seq_of(x, y, k):
    return (x * 4 + y) * 2 + k


def remote(src, dst, send, recv, seq, head):
    return pltpu.make_async_remote_copy(
        src_ref=src,
        dst_ref=dst,
        send_sem=send,
        recv_sem=recv,
        device_id={"seq": seq, "head": head},
        device_id_type=MESH,
    )


def barrier_with(peers):
    barrier = pltpu.get_barrier_semaphore()
    for seq, head in peers:
        pl.semaphore_signal(
            barrier, inc=1, device_id={"seq": seq, "head": head}, device_id_type=MESH
        )
    pl.semaphore_wait(barrier, len(peers))


def block_rows(s):
    return pl.ds(pl.multiple_of(s * ROWS, 128), ROWS)


def head_cols(y):
    return pl.ds(pl.multiple_of(y * HD, HD), HD)


def tile_of(d, t):
    return 4 * t + d + (t % 2) * (3 - 2 * d)


def slot_of(x, y, k, j):
    u = 3 * k + j
    tile = 3 * (4 * x + y) + u // 2
    t, r = tile // 4, tile % 4
    return r + (t % 2) * (3 - 2 * r), 2 * t + u % 2


def gather_kernel(
    q_ref, k_ref, v_ref, og_hbm, w_hbm, doc_ref,
    ko, vo, qo, do, doco,
    land, w_ref, acc, grad,
    g_send, g_recv, y_send, y_recv, sib_send, sib_recv, x_send, x_recv,
    q_send, q_recv, o_send, o_recv, d_send, d_recv, w_sem, l_sem,
):
    s, g, x, y, k = place()
    xh, z = g // 4, g % 4
    up = xh * 4 + (z + 1) % 4
    down = xh * 4 + (z + 3) % 4
    across = (1 - xh) * 4 + z
    sibling = seq_of(x, y, 1 - k)
    other = seq_of(1 - x, y, k)

    og_ref = land.at[0]
    og_copy = pltpu.make_async_copy(og_hbm, og_ref, g_recv.at[0, 0])
    og_copy.start()
    w_copy = pltpu.make_async_copy(w_hbm, w_ref, w_sem)
    w_copy.start()
    barrier_with(
        [((s + i) % 16, g) for i in range(1, 16)] + [(s, up), (s, down), (s, across)]
    )
    og_copy.wait()

    sends = []

    def go(copy):
        copy.start()
        sends.append(copy)

    def rows(c):
        return pl.ds(c * CH, CH)

    order = [(0, 2), (1, 3), (2, 0), (3, 1)]

    def ring(n, src, slot, c, head):
        return remote(src, land.at[slot, rows(c)], g_send.at[n, c], g_recv.at[slot, c], s, head)

    for up_c, down_c in order:
        go(ring(0, og_ref.at[rows(up_c)], 1, up_c, up))
        go(ring(1, og_ref.at[rows(down_c)], 2, down_c, down))
        go(ring(2, og_ref.at[rows(up_c)], 4, up_c, across))

    mine = block_rows(s)
    local = []
    for i, (src, dst) in enumerate(((k_ref, ko), (v_ref, vo))):
        copy = pltpu.make_async_copy(src.at[:, head_cols(y)], dst.at[mine], l_sem.at[i])
        copy.start()
        local.append(copy)
    for dy in (2, 1, 3):
        ty = (y + dy) % 4
        for i, (src, dst) in enumerate(((k_ref, ko), (v_ref, vo))):
            go(remote(src.at[:, head_cols(ty)], dst.at[mine], y_send.at[dy, i],
                      y_recv.at[dy, i], seq_of(x, ty, k), g))

    def x_copy(src, dst, where, dy, i):
        return remote(src, dst.at[where], x_send.at[dy, i], x_recv.at[dy, i], other, g)

    def sib_copy(src, dst, where, n, i):
        return remote(src, dst.at[where], sib_send.at[n, i], sib_recv.at[n, i], sibling, g)

    for i, (src, dst) in enumerate(((k_ref, ko), (v_ref, vo))):
        go(sib_copy(src.at[:, head_cols(y)], dst, mine, 0, i))

        go(x_copy(src.at[:, head_cols(y)], dst, mine, 0, i))

    def spread(src, dst, send, recv):
        for dy in (2, 1, 3, 0):
            ty = (y + dy) % 4
            for j in range(3):
                d, slot = slot_of(x, y, k, j)
                piece = src.at[pl.ds(j * HD, HD), head_cols(ty)]
                there = dst.at[pl.ds(pl.multiple_of(slot * HD, HD), HD)]
                if dy:
                    go(remote(piece, there, send.at[dy, j], recv.at[slot], seq_of(d // 2, ty, d % 2), g))
                else:
                    @pl.when(d != 2 * x + k)
                    def _():
                        remote(piece, there, send.at[0, j], recv.at[slot],
                               seq_of(d // 2, y, d % 2), g).start()

                    @pl.when(d == 2 * x + k)
                    def _():
                        pltpu.make_async_copy(piece, there, recv.at[slot]).start()

    def drain(src, dst, send, recv):
        for j in range(3):
            d, slot = slot_of(x, y, k, j)
            piece = src.at[pl.ds(j * HD, HD), head_cols(y)]
            there = dst.at[pl.ds(pl.multiple_of(slot * HD, HD), HD)]

            @pl.when(d != 2 * x + k)
            def _():
                remote(piece, there, send.at[0, j], recv.at[slot],
                       seq_of(d // 2, y, d % 2), g).wait_send()
        for slot in range(12):
            there = dst.at[pl.ds(slot * HD, HD)]
            pltpu.make_async_copy(there, there, recv.at[slot]).wait()

    spread(q_ref, qo, q_send, q_recv)
    for i in range(1, 16):
        go(remote(doc_ref, doco.at[s], d_send.at[i], d_recv.at[i], (s + i) % 16, g))
    own_doc = pltpu.make_async_copy(doc_ref, doco.at[s], d_recv.at[0])
    own_doc.start()

    def got(slot, c):
        ring(0, land.at[slot, rows(c)], slot, c, up).wait_recv()

    def relay_kv(dy):
        where = block_rows(seq_of(x, (y + 4 - dy) % 4, k))
        for i, dst in enumerate((ko, vo)):
            remote(dst.at[where], dst.at[where], y_send.at[dy, i], y_recv.at[dy, i], sibling, g).wait_recv()
            go(x_copy(dst.at[where], dst, where, dy, i))
            go(sib_copy(dst.at[where], dst, where, dy, i))

    def from_x(dy):
        where = block_rows(seq_of(1 - x, (y + 4 - dy) % 4, k))
        for i, dst in enumerate((ko, vo)):
            x_copy(dst.at[where], dst, where, dy, i).wait_recv()
            go(sib_copy(dst.at[where], dst, where, 4 + dy, i))

    for c in (0, 1):
        got(1, c)
        go(ring(3, land.at[1, rows(c)], 3, c, up))
        got(2, c + 2)
        go(ring(3, land.at[2, rows(c + 2)], 3, c + 2, down))
    relay_kv(1)
    relay_kv(3)
    for c in (0, 1):
        got(4, c)
        go(ring(4, land.at[4, rows(c)], 5, c, up))
        go(ring(5, land.at[4, rows(c)], 6, c, down))
    relay_kv(2)
    for c in (2, 3):
        got(4, c)
        go(ring(4, land.at[4, rows(c)], 5, c, up))
        go(ring(5, land.at[4, rows(c)], 6, c, down))
    from_x(0)

    w_copy.wait()

    def product(slot, head):
        block = land[slot]
        weights = w_ref[:, pl.ds(pl.multiple_of(head * COLS, COLS), COLS)]
        part = lax.dot_general(block, weights, NT, preferred_element_type=jnp.float32)
        acc[...] = part if slot == 0 else acc[...] + part

    far = xh * 4 + (z + 2) % 4
    product(0, g)
    for c in (2, 3):
        got(1, c)
        got(2, c - 2)
    product(1, down)
    product(2, up)
    for c in range(4):
        got(3, c)
    product(3, far)
    product(4, across)
    from_x(1)
    for c in (0, 1):
        got(5, c)
        go(ring(6, land.at[5, rows(c)], 7, c, up))
    from_x(3)
    for c in (2, 3):
        got(6, c)
        go(ring(6, land.at[6, rows(c)], 7, c, down))
    from_x(2)
    turn = (1 - xh) * 4
    for c in (2, 3):
        got(5, c)
    product(5, turn + (z + 3) % 4)
    for c in (0, 1):
        got(6, c)
    product(6, turn + (z + 1) % 4)
    for c in range(4):
        got(7, c)
    product(7, turn + (z + 2) % 4)
    grad[...] = acc[...].astype(jnp.bfloat16)
    spread(grad, do, o_send, o_recv)

    for copy in local:
        copy.wait()
    own_doc.wait()
    for i in range(1, 16):
        remote(doc_ref, doco.at[(s + 16 - i) % 16], d_send.at[i], d_recv.at[i], s, g).wait_recv()
    for dy in range(4):
        where = block_rows(seq_of(x, (y + 4 - dy) % 4, 1 - k))
        for i, dst in enumerate((ko, vo)):
            sib_copy(dst.at[where], dst, where, dy, i).wait_recv()

    for dy in range(4):
        where = block_rows(seq_of(1 - x, (y + 4 - dy) % 4, 1 - k))
        for i, dst in enumerate((ko, vo)):
            sib_copy(dst.at[where], dst, where, 4 + dy, i).wait_recv()
    drain(q_ref, qo, q_send, q_recv)
    drain(grad, do, o_send, o_recv)
    for copy in sends:
        copy.wait_send()


def gather_call(queries, keys_in, values, out_grad, out_weight, docs):
    hbm = pl.BlockSpec(memory_space=pltpu.HBM)
    anyspace = pl.BlockSpec(memory_space=pl.ANY)
    dma = pltpu.SemaphoreType.DMA
    bf = jnp.bfloat16
    return pl.pallas_call(
        gather_kernel,
        out_shape=(
            jax.ShapeDtypeStruct((TOTAL, HD), bf),
            jax.ShapeDtypeStruct((TOTAL, HD), bf),
            jax.ShapeDtypeStruct((QLOCAL, HD), bf),
            jax.ShapeDtypeStruct((QLOCAL, HD), bf),
            jax.ShapeDtypeStruct((16, 3, HD), jnp.int32),
        ),
        in_specs=[hbm] * 6,
        out_specs=(anyspace,) * 5,
        scratch_shapes=[
            pltpu.VMEM((8, ROWS, COLS), bf),
            pltpu.VMEM((COLS, 4096), bf),
            pltpu.VMEM((ROWS, COLS), jnp.float32),
            pltpu.VMEM((ROWS, COLS), bf),
            dma((7, NCH)), dma((8, NCH)), dma((4, 2)), dma((4, 2)),
            dma((8, 2)), dma((8, 2)), dma((4, 2)), dma((4, 2)),
            dma((4, 3)), dma((12,)), dma((4, 3)), dma((12,)),
            dma((16,)), dma((16,)), dma, dma((2,)),
        ],
        compiler_params=pltpu.CompilerParams(
            collective_id=0, has_side_effects=True, vmem_limit_bytes=12 << 20
        ),
        name="spread_rows",
    )(
        *(
            pltpu.with_memory_space_constraint(a, pltpu.HBM)
            for a in (queries, keys_in, values, out_grad, out_weight, docs)
        )
    )


def attention_kernel(
    doc_v, q_ref, o_ref, k_ref, v_ref,
    dq_ref, dk_ref, dv_ref,
    p_buf, g_buf, dk_acc, dv_acc, dq_acc,
):
    s, g, x, y, k = place()
    docs = doc_v[...]
    starts = [jnp.int32(0)]
    for d in range(1, 8):
        starts.append(jnp.sum(jnp.where(docs < d, 1, 0)))
    dk_acc[...] = jnp.zeros_like(dk_acc)
    dv_acc[...] = jnp.zeros_like(dv_acc)
    factor = SCALE * LOG2E
    lane = lax.broadcasted_iota(jnp.int32, (1, QT), 1)
    sub = lax.broadcasted_iota(jnp.int32, (KT, QT), 0)
    f32 = jnp.float32

    def folded(value, reduce):
        return reduce(value.reshape(KT // 8, 8, QT), axis=0)

    @pl.loop(0, QLOCAL // QT)
    def _(t):
        q0 = pl.multiple_of(QT * tile_of(2 * x + k, t), QT)
        mine = pl.ds(pl.multiple_of(t * QT, QT), QT)
        q_tile = q_ref[mine, :]
        o_tile = o_ref[mine, :]
        diagonal = q0 // KT
        row = q0 // HD
        doc_q = jnp.concatenate(
            [doc_v[u // 3, pl.ds(u % 3, 1), :] for u in (row, row + 1)], axis=1
        )
        start = jnp.zeros((1, QT), jnp.int32)
        for d in range(1, 8):
            start = jnp.where(doc_q == d, starts[d], start)
        k_low = jnp.min(start) // KT
        k_full = jnp.minimum((jnp.max(start) + KT - 1) // KT, diagonal)
        pos = q0 + lane

        def rows_of(kt):
            return pl.ds(pl.multiple_of(kt * KT, KT), KT)

        def plain(kt, top):
            scores = lax.dot_general(k_ref[rows_of(kt), :], q_tile, NT, preferred_element_type=f32)
            p_buf[kt] = scores
            return jnp.maximum(top, folded(scores, jnp.max))

        def masked(kt, top):
            scores = lax.dot_general(k_ref[rows_of(kt), :], q_tile, NT, preferred_element_type=f32)
            key = kt * KT + sub
            scores = jnp.where((key >= start) & (key <= pos), scores, NEG)
            p_buf[kt] = scores
            return jnp.maximum(top, folded(scores, jnp.max))

        top = jnp.full((8, QT), NEG, f32)
        top = lax.fori_loop(k_low, k_full, masked, top)
        top = lax.fori_loop(k_full, diagonal, plain, top)
        top = jnp.max(masked(diagonal, top), axis=0, keepdims=True)

        def weigh(kt, carry):
            total, weighted = carry
            p = jnp.exp2((p_buf[kt] - top) * factor)
            gp = lax.dot_general(v_ref[rows_of(kt), :], o_tile, NT, preferred_element_type=f32)
            p_buf[kt] = p
            g_buf[kt] = gp
            return total + folded(p, jnp.sum), weighted + folded(p * gp, jnp.sum)

        zero = jnp.zeros((8, QT), f32)
        total, weighted = lax.fori_loop(k_low, diagonal + 1, weigh, (zero, zero))
        inverse = 1.0 / jnp.sum(total, axis=0, keepdims=True)
        dot_row = jnp.sum(weighted, axis=0, keepdims=True) * inverse
        dq_acc[...] = jnp.zeros_like(dq_acc)

        @pl.loop(k_low, diagonal + 1)
        def _(kt):
            keys = rows_of(kt)
            probs = p_buf[kt] * inverse
            ds = (probs * (g_buf[kt] - dot_row)).astype(jnp.bfloat16)
            dv_acc[keys, :] += lax.dot_general(
                probs.astype(jnp.bfloat16), o_tile, NN, preferred_element_type=f32
            )
            dk_acc[keys, :] += lax.dot_general(ds, q_tile, NN, preferred_element_type=f32)
            dq_acc[...] += lax.dot_general(ds, k_ref[keys, :], TN, preferred_element_type=f32)

        dq_ref[mine, :] = (dq_acc[...] * SCALE).astype(jnp.bfloat16)

    dk_ref[...] = (dk_acc[...] * SCALE).astype(jnp.bfloat16)
    dv_ref[...] = dv_acc[...].astype(jnp.bfloat16)


def attention_call(docs, q, o, k, v):
    vm = pl.BlockSpec(memory_space=pltpu.VMEM)
    bf, f32 = jnp.bfloat16, jnp.float32
    tiles = TOTAL // KT
    return pl.pallas_call(
        attention_kernel,
        out_shape=(
            jax.ShapeDtypeStruct((QLOCAL, HD), bf),
            jax.ShapeDtypeStruct((TOTAL, HD), bf),
            jax.ShapeDtypeStruct((TOTAL, HD), bf),
        ),
        in_specs=[vm] * 5,
        out_specs=(vm, vm, vm),
        scratch_shapes=[
            pltpu.VMEM((tiles, KT, QT), f32),
            pltpu.VMEM((tiles, KT, QT), f32),
            pltpu.VMEM((TOTAL, HD), f32),
            pltpu.VMEM((TOTAL, HD), f32),
            pltpu.VMEM((QT, HD), f32),
        ],
        compiler_params=pltpu.CompilerParams(vmem_limit_bytes=32 << 20),
        name="attention_grads",
    )(docs, q, o, k, v)


def return_kernel(
    dq_ref, dk_ref, dv_ref,
    qo, ko, vo,
    sib_buf, x_buf, stage,
    q_send, q_recv, sib_send, sib_recv, x_send, x_recv, y_send, y_recv,
):
    s, g, x, y, k = place()
    sibling = seq_of(x, y, 1 - k)
    other = seq_of(1 - x, y, k)
    barrier_with([((s + i) % 16, g) for i in range(1, 16)])
    parts = (dk_ref, dv_ref)
    outs = (ko, vo)
    order = (2, 1, 3, 0)

    def column(n):
        return 1 - x if n < 4 else x

    def sib_copy(n, i):
        src = parts[i].at[block_rows(seq_of(column(n), (y + n) % 4, 1 - k))]
        return remote(src, sib_buf.at[n, i], sib_send.at[n, i], sib_recv.at[n, i], sibling, g)

    def x_copy(dy, i):
        return remote(stage.at[dy, i], x_buf.at[dy, i], x_send.at[dy, i], x_recv.at[dy, i], other, g)

    def y_copy(dy, i):
        return remote(
            stage.at[4 + dy, i], outs[i].at[:, head_cols(y)], y_send.at[dy, i], y_recv.at[dy, i],
            seq_of(x, (y + dy) % 4, k), g,
        )

    for dy in order:
        for i in range(2):
            sib_copy(dy, i).start()

    def q_piece(n):
        tile = tile_of(2 * x + k, n // 2)
        chip, u = tile // 3, (tile % 3) * 2 + n % 2
        tk, j = u // 3, u % 3
        src = dq_ref.at[pl.ds(n * HD, HD)]
        dst = qo.at[pl.ds(pl.multiple_of(j * HD, HD), HD), head_cols(y)]
        return chip * 2 + tk, j, src, dst

    for n in range(12):
        to, j, src, dst = q_piece(n)

        @pl.when(to == s)
        def _():
            pltpu.make_async_copy(src, dst, q_recv.at[y, j]).start()

        @pl.when(to != s)
        def _():
            remote(src, dst, q_send.at[n], q_recv.at[y, j], to, g).start()

    for dy in order:
        for i in range(2):
            sib_copy(4 + dy, i).start()

    def summed(n, i):
        sib_copy(n, i).wait_recv()
        rows = block_rows(seq_of(column(n), (y + n) % 4, k))
        total = parts[i][rows, :].astype(jnp.float32) + sib_buf[n, i].astype(jnp.float32)
        if n >= 4:
            x_copy(n - 4, i).wait_recv()
            total = total + x_buf[n - 4, i].astype(jnp.float32)
        stage[n, i] = total.astype(jnp.bfloat16)

    for dy in order:
        for i in range(2):
            summed(dy, i)
            x_copy(dy, i).start()
    for dy in order:
        for i in range(2):
            summed(4 + dy, i)
            if dy:
                y_copy(dy, i).start()
            else:
                pltpu.make_async_copy(
                    stage.at[4, i], outs[i].at[:, head_cols(y)], y_recv.at[0, i]
                ).start()

    for ty in range(4):
        for j in range(3):
            dst = qo.at[pl.ds(j * HD, HD), pl.ds(ty * HD, HD)]
            pltpu.make_async_copy(dst, dst, q_recv.at[ty, j]).wait()
    for n in range(12):
        to, j, src, dst = q_piece(n)

        @pl.when(to != s)
        def _():
            remote(src, dst, q_send.at[n], q_recv.at[y, j], to, g).wait_send()
    for dy in range(4):
        for i in range(2):
            dst = outs[i].at[:, head_cols((y + 4 - dy) % 4)]
            pltpu.make_async_copy(dst, dst, y_recv.at[dy, i]).wait()
            sib_copy(dy, i).wait_send()
            sib_copy(4 + dy, i).wait_send()
            x_copy(dy, i).wait_send()
            if dy:
                y_copy(dy, i).wait_send()


def return_call(dq, dk, dv):
    vm = pl.BlockSpec(memory_space=pltpu.VMEM)
    anyspace = pl.BlockSpec(memory_space=pl.ANY)
    dma = pltpu.SemaphoreType.DMA
    bf = jnp.bfloat16
    return pl.pallas_call(
        return_kernel,
        out_shape=(jax.ShapeDtypeStruct((ROWS, COLS), bf),) * 3,
        in_specs=[vm, vm, vm],
        out_specs=(anyspace,) * 3,
        scratch_shapes=[
            pltpu.VMEM((8, 2, ROWS, HD), bf),
            pltpu.VMEM((4, 2, ROWS, HD), bf),
            pltpu.VMEM((8, 2, ROWS, HD), bf),
            dma((12,)), dma((4, 3)), dma((8, 2)), dma((8, 2)),
            dma((4, 2)), dma((4, 2)), dma((4, 2)), dma((4, 2)),
        ],
        compiler_params=pltpu.CompilerParams(
            collective_id=1, has_side_effects=True, vmem_limit_bytes=8 << 20
        ),
        name="return_grads",
    )(dq, dk, dv)


def store_kernel(a, b, c, ao, bo, co, sem):
    copies = [
        pltpu.make_async_copy(src, dst, sem.at[i])
        for i, (src, dst) in enumerate(((a, ao), (b, bo), (c, co)))
    ]
    for copy in copies:
        copy.start()
    for copy in copies:
        copy.wait()


def store_call(*arrays):
    vm = pl.BlockSpec(memory_space=pltpu.VMEM)
    hbm = pl.BlockSpec(memory_space=pltpu.HBM)
    return pl.pallas_call(
        store_kernel,
        out_shape=(jax.ShapeDtypeStruct((ROWS, COLS), jnp.bfloat16),) * 3,
        in_specs=[vm] * 3,
        out_specs=(hbm,) * 3,
        scratch_shapes=[pltpu.SemaphoreType.DMA((3,))],
        compiler_params=pltpu.CompilerParams(vmem_limit_bytes=4 << 20),
        name="store_grads",
    )(*arrays)


def per_device(queries, keys_in, values, out_grad, out_weight, doc_ids):
    k, v, q, o, docs = gather_call(
        queries, keys_in, values, out_grad, out_weight, doc_ids.reshape(3, HD)
    )
    dq, dk, dv = attention_call(docs, q, o, k, v)
    return store_call(*return_call(dq, dk, dv))


def solution(mesh):
    in_specs = (
        P("seq", "head"),
        P("seq", "head"),
        P("seq", "head"),
        P("seq", "head"),
        P("head", None),
        P("seq"),
    )
    out_specs = (P("seq", "head"), P("seq", "head"), P("seq", "head"))
    return jax.shard_map(
        per_device, mesh=mesh, in_specs=in_specs, out_specs=out_specs, check_vma=False
    )
```

```python
import functools

import jax
import jax.numpy as jnp
from jax import lax
from jax.experimental import pallas as pl
from jax.experimental.pallas import tpu as pltpu
from jax.sharding import PartitionSpec as P

HD = 128
ROWS = 384
COLS = 512
HEADS_LOCAL = 4
TOTAL = 6144
QT = 256
KT = 512
QLOCAL = 1536
NCH = 6
CH = ROWS // NCH
NEG = -1e30
SCALE = HD ** -0.5
LOG2E = 1.4426950408889634
MESH = pl.DeviceIdType.MESH
NT = (((1,), (1,)), ((), ()))
TN = (((0,), (0,)), ((), ()))
NN = (((1,), (0,)), ((), ()))


def place():
    s = lax.axis_index("seq")
    g = lax.axis_index("head")
    x = s // 8
    y = (s // 2) % 4
    k = s % 2
    return s, g, x, y, k


def seq_of(x, y, k):
    return (x * 4 + y) * 2 + k


def remote(src, dst, send, recv, seq, head):
    return pltpu.make_async_remote_copy(
        src_ref=src,
        dst_ref=dst,
        send_sem=send,
        recv_sem=recv,
        device_id={"seq": seq, "head": head},
        device_id_type=MESH,
    )


def barrier_with(peers):
    barrier = pltpu.get_barrier_semaphore()
    for seq, head in peers:
        pl.semaphore_signal(
            barrier, inc=1, device_id={"seq": seq, "head": head}, device_id_type=MESH
        )
    pl.semaphore_wait(barrier, len(peers))


def block_rows(s):
    return pl.ds(pl.multiple_of(s * ROWS, 128), ROWS)


def head_cols(y):
    return pl.ds(pl.multiple_of(y * HD, HD), HD)


def tile_of(x, k, t):
    return 12 * x + 2 * t + k + (t % 2) * (1 - 2 * k)


def slot_of(y, k, j):
    u = 3 * k + j
    tile = 3 * y + u // 2
    t, r = tile // 2, tile % 2
    return r + (t % 2) * (1 - 2 * r), 2 * t + u % 2


def gather_kernel(
    q_ref, k_ref, v_ref, og_hbm, w_hbm, doc_ref,
    ko, vo, qo, do, doco,
    land, w_ref, acc, grad,
    g_send, g_recv, y_send, y_recv, sib_send, sib_recv, x_send, x_recv,
    q_send, q_recv, o_send, o_recv, d_send, d_recv, w_sem, l_sem,
):
    s, g, x, y, k = place()
    xh, z = g // 4, g % 4
    up = xh * 4 + (z + 1) % 4
    down = xh * 4 + (z + 3) % 4
    across = (1 - xh) * 4 + z
    sibling = seq_of(x, y, 1 - k)
    other = seq_of(1 - x, y, k)

    og_copy = pltpu.make_async_copy(og_hbm, land.at[0], g_recv.at[0, 0])
    og_copy.start()
    w_copy = pltpu.make_async_copy(w_hbm, w_ref, w_sem)
    w_copy.start()
    barrier_with(
        [((s + i) % 16, g) for i in range(1, 16)] + [(s, up), (s, down), (s, across)]
    )

    sends = []

    def go(copy):
        copy.start()
        sends.append(copy)

    def rows(c):
        return pl.ds(c * CH, CH)

    order = ((0, 5), (1, 4), (2, 3), (3, 2), (4, 1), (5, 0))

    def ring(n, src, slot, c, head):
        return remote(src, land.at[slot, rows(c)], g_send.at[n, c], g_recv.at[slot, c], s, head)

    for (up_c, down_c), across_c in zip(order, (0, 5, 1, 4, 2, 3)):
        go(ring(0, og_hbm.at[rows(up_c)], 1, up_c, up))
        go(ring(1, og_hbm.at[rows(down_c)], 2, down_c, down))
        go(ring(2, og_hbm.at[rows(across_c)], 4, across_c, across))

    mine = block_rows(s)
    local = []
    for i, (src, dst) in enumerate(((k_ref, ko), (v_ref, vo))):
        copy = pltpu.make_async_copy(src.at[:, head_cols(y)], dst.at[mine], l_sem.at[i])
        copy.start()
        local.append(copy)
    for dy in (2, 1, 3):
        ty = (y + dy) % 4
        for i, (src, dst) in enumerate(((k_ref, ko), (v_ref, vo))):
            go(remote(src.at[:, head_cols(ty)], dst.at[mine], y_send.at[dy, i],
                      y_recv.at[dy, i], seq_of(x, ty, k), g))

    def x_copy(src, dst, where, dy, i):
        return remote(src, dst.at[where], x_send.at[dy, i], x_recv.at[dy, i], other, g)

    def sib_copy(src, dst, where, n, i):
        return remote(src, dst.at[where], sib_send.at[n, i], sib_recv.at[n, i], sibling, g)

    for i, (src, dst) in enumerate(((k_ref, ko), (v_ref, vo))):
        go(sib_copy(src.at[:, head_cols(y)], dst, mine, 0, i))


    def spread(src, dst, send, recv, pieces=(0, 2, 1)):
        for dy in (2, 1, 3, 0):
            ty = (y + dy) % 4
            for j in pieces:
                core, slot = slot_of(y, k, j)
                piece = src.at[pl.ds(j * HD, HD), head_cols(ty)]
                there = dst.at[pl.ds(pl.multiple_of(slot * HD, HD), HD)]
                if dy:
                    go(remote(piece, there, send.at[dy, j], recv.at[slot], seq_of(x, ty, core), g))
                else:
                    @pl.when(core != k)
                    def _():
                        remote(piece, there, send.at[0, j], recv.at[slot],
                               sibling, g).start()

                    @pl.when(core == k)
                    def _():
                        pltpu.make_async_copy(piece, there, recv.at[slot]).start()

    def drain(src, dst, send, recv):
        for j in range(3):
            core, slot = slot_of(y, k, j)
            piece = src.at[pl.ds(j * HD, HD), head_cols(y)]
            there = dst.at[pl.ds(pl.multiple_of(slot * HD, HD), HD)]

            @pl.when(core != k)
            def _():
                remote(piece, there, send.at[0, j], recv.at[slot],
                       sibling, g).wait_send()
        for slot in range(12):
            there = dst.at[pl.ds(slot * HD, HD)]
            pltpu.make_async_copy(there, there, recv.at[slot]).wait()

    for i in range(1, 16):
        go(remote(doc_ref, doco.at[s], d_send.at[i], d_recv.at[i], (s + i) % 16, g))
    own_doc = pltpu.make_async_copy(doc_ref, doco.at[s], d_recv.at[0])
    own_doc.start()

    def got(slot, c):
        ring(0, land.at[slot, rows(c)], slot, c, up).wait_recv()

    def relay_kv(dy):
        where = block_rows(seq_of(x, (y + 4 - dy) % 4, k))
        for i, dst in enumerate((ko, vo)):
            remote(dst.at[where], dst.at[where], y_send.at[dy, i], y_recv.at[dy, i], sibling, g).wait_recv()
            go(sib_copy(dst.at[where], dst, where, dy, i))

    def from_x(dy):
        where = block_rows(seq_of(0, (y + 4 - dy) % 4, k))

        @pl.when(x == 1)
        def _():
            for i, dst in enumerate((ko, vo)):
                x_copy(dst.at[where], dst, where, dy, i).wait_recv()
                sib_copy(dst.at[where], dst, where, 4 + dy, i).start()

    def pass_on(slot):
        for c, e in order[:3]:
            got(slot, c)
            go(ring(slot + 2, land.at[slot, rows(c)], slot + 2, c, up))
            got(slot + 1, e)
            go(ring(slot + 2, land.at[slot + 1, rows(e)], slot + 2, e, down))

    def share(c):
        got(4, c)
        go(ring(4, land.at[4, rows(c)], 5, c, up))
        go(ring(5, land.at[4, rows(c)], 6, c, down))

    pass_on(1)
    share(0)
    relay_kv(1)
    share(5)
    relay_kv(3)
    share(1)
    share(4)
    relay_kv(2)
    share(2)
    share(3)
    @pl.when(x == 0)
    def _():
        for i, (src, dst) in enumerate(((k_ref, ko), (v_ref, vo))):
            x_copy(src.at[:, head_cols(y)], dst, mine, 0, i).start()
        for dy in (1, 3, 2):
            where = block_rows(seq_of(0, (y + 4 - dy) % 4, k))
            for i, dst in enumerate((ko, vo)):
                x_copy(dst.at[where], dst, where, dy, i).start()
    spread(q_ref, qo, q_send, q_recv)

    w_copy.wait()

    def product(slot, head):
        block = land[slot]
        weights = w_ref[:, pl.ds(pl.multiple_of(head * COLS, COLS), COLS)]
        part = lax.dot_general(block, weights, NT, preferred_element_type=jnp.float32)
        acc[...] = part if slot == 0 else acc[...] + part

    far = xh * 4 + (z + 2) % 4
    turn = (1 - xh) * 4
    og_copy.wait()
    product(0, g)
    for c, e in order[:3]:
        got(1, e)
        got(2, c)
    product(1, down)
    product(2, up)
    from_x(0)
    for c, e in order[:3]:
        got(3, c)
        got(3, e)
    product(3, far)
    product(4, across)
    pass_on(5)
    from_x(1)
    for c, e in order[:3]:
        got(5, e)
        got(6, c)
    product(5, turn + (z + 3) % 4)
    product(6, turn + (z + 1) % 4)
    from_x(3)

    last = turn + (z + 2) % 4
    weights = w_ref[:, pl.ds(pl.multiple_of(last * COLS, COLS), COLS)]

    def finish(j):
        piece = pl.ds(j * HD, HD)
        part = lax.dot_general(land[7, piece], weights, NT, preferred_element_type=jnp.float32)
        grad[piece] = (acc[piece] + part).astype(jnp.bfloat16)
        spread(grad, do, o_send, o_recv, (j,))

    for c, e in order[:2]:
        got(7, c)
        got(7, e)
    finish(0)
    finish(2)
    for c in (2, 3):
        got(7, c)
    finish(1)
    from_x(2)

    for copy in local:
        copy.wait()
    own_doc.wait()
    for i in range(1, 16):
        remote(doc_ref, doco.at[(s + 16 - i) % 16], d_send.at[i], d_recv.at[i], s, g).wait_recv()
    for dy in range(4):
        where = block_rows(seq_of(x, (y + 4 - dy) % 4, 1 - k))
        for i, dst in enumerate((ko, vo)):
            sib_copy(dst.at[where], dst, where, dy, i).wait_recv()

    @pl.when(x == 0)
    def _():
        for dy in range(4):
            where = block_rows(seq_of(0, (y + 4 - dy) % 4, k))
            for i, dst in enumerate((ko, vo)):
                x_copy(dst.at[where], dst, where, dy, i).wait_send()

    @pl.when(x == 1)
    def _():
        for dy in range(4):
            where = block_rows(seq_of(0, (y + 4 - dy) % 4, 1 - k))
            for i, dst in enumerate((ko, vo)):
                copy = sib_copy(dst.at[where], dst, where, 4 + dy, i)
                copy.wait_recv()
                copy.wait_send()
    drain(q_ref, qo, q_send, q_recv)
    drain(grad, do, o_send, o_recv)
    for copy in sends:
        copy.wait_send()


def gather_call(queries, keys_in, values, out_grad, out_weight, docs):
    hbm = pl.BlockSpec(memory_space=pltpu.HBM)
    anyspace = pl.BlockSpec(memory_space=pl.ANY)
    dma = pltpu.SemaphoreType.DMA
    bf = jnp.bfloat16
    return pl.pallas_call(
        gather_kernel,
        out_shape=(
            jax.ShapeDtypeStruct((TOTAL, HD), bf),
            jax.ShapeDtypeStruct((TOTAL, HD), bf),
            jax.ShapeDtypeStruct((QLOCAL, HD), bf),
            jax.ShapeDtypeStruct((QLOCAL, HD), bf),
            jax.ShapeDtypeStruct((16, 3, HD), jnp.int32),
        ),
        in_specs=[hbm] * 6,
        out_specs=(anyspace,) * 5,
        scratch_shapes=[
            pltpu.VMEM((8, ROWS, COLS), bf),
            pltpu.VMEM((COLS, 4096), bf),
            pltpu.VMEM((ROWS, COLS), jnp.float32),
            pltpu.VMEM((ROWS, COLS), bf),
            dma((8, NCH)), dma((8, NCH)), dma((4, 2)), dma((4, 2)),
            dma((8, 2)), dma((8, 2)), dma((4, 2)), dma((4, 2)),
            dma((4, 3)), dma((12,)), dma((4, 3)), dma((12,)),
            dma((16,)), dma((16,)), dma, dma((2,)),
        ],
        compiler_params=pltpu.CompilerParams(
            collective_id=0, has_side_effects=True, vmem_limit_bytes=12 << 20
        ),
        name="spread_rows",
    )(
        *(
            pltpu.with_memory_space_constraint(a, pltpu.HBM)
            for a in (queries, keys_in, values, out_grad, out_weight, docs)
        )
    )


def attention_kernel(
    doc_v, q_ref, o_ref, k_ref, v_ref,
    dq_ref, dk_ref, dv_ref,
    p_buf, g_buf, dk_acc, dv_acc, dq_acc, k_turn,
):
    s, g, x, y, k = place()
    docs = doc_v[...]
    starts = [jnp.int32(0)]
    for d in range(1, 8):
        starts.append(jnp.sum(jnp.where(docs < d, 1, 0)))
    dk_acc[...] = jnp.zeros_like(dk_acc)
    dv_acc[...] = jnp.zeros_like(dv_acc)
    for n in range(TOTAL // 256):
        k_turn[:, n * 256:(n + 1) * 256] = k_ref[n * 256:(n + 1) * 256, :].T
    factor = SCALE * LOG2E
    lane = lax.broadcasted_iota(jnp.int32, (1, QT), 1)
    sub = lax.broadcasted_iota(jnp.int32, (KT, QT), 0)
    f32 = jnp.float32

    def folded(value, reduce):
        return reduce(value.reshape(KT // 8, 8, QT), axis=0)

    @pl.loop(0, QLOCAL // QT)
    def _(t):
        q0 = pl.multiple_of(QT * tile_of(x, k, t), QT)
        mine = pl.ds(pl.multiple_of(t * QT, QT), QT)
        q_tile = q_ref[mine, :]
        o_tile = o_ref[mine, :]
        diagonal = q0 // KT
        row = q0 // HD
        doc_q = jnp.concatenate(
            [doc_v[u // 3, pl.ds(u % 3, 1), :] for u in (row, row + 1)], axis=1
        )
        start = jnp.zeros((1, QT), jnp.int32)
        for d in range(1, 8):
            start = jnp.where(doc_q == d, starts[d], start)
        k_low = jnp.min(start) // KT
        k_full = jnp.minimum((jnp.max(start) + KT - 1) // KT, diagonal)
        pos = q0 + lane

        def rows_of(kt):
            return pl.ds(pl.multiple_of(kt * KT, KT), KT)

        def plain(kt, top):
            scores = lax.dot_general(k_ref[rows_of(kt), :], q_tile, NT, preferred_element_type=f32)
            p_buf[kt] = scores
            return jnp.maximum(top, folded(scores, jnp.max))

        def masked(kt, top):
            scores = lax.dot_general(k_ref[rows_of(kt), :], q_tile, NT, preferred_element_type=f32)
            key = kt * KT + sub
            scores = jnp.where((key >= start) & (key <= pos), scores, NEG)
            p_buf[kt] = scores
            return jnp.maximum(top, folded(scores, jnp.max))

        top = jnp.full((8, QT), NEG, f32)
        top = lax.fori_loop(k_low, k_full, masked, top)
        top = lax.fori_loop(k_full, diagonal, plain, top)
        top = jnp.max(masked(diagonal, top), axis=0, keepdims=True)

        def weigh(kt, carry):
            total, weighted = carry
            p = jnp.exp2((p_buf[kt] - top) * factor)
            gp = lax.dot_general(v_ref[rows_of(kt), :], o_tile, NT, preferred_element_type=f32)
            p_buf[kt] = p
            g_buf[kt] = gp
            return total + folded(p, jnp.sum), weighted + folded(p * gp, jnp.sum)

        zero = jnp.zeros((8, QT), f32)
        total, weighted = lax.fori_loop(k_low, diagonal + 1, weigh, (zero, zero))
        inverse = 1.0 / jnp.sum(total, axis=0, keepdims=True)
        dot_row = jnp.sum(weighted, axis=0, keepdims=True) * inverse
        dq_acc[...] = jnp.zeros_like(dq_acc)

        @pl.loop(k_low, diagonal + 1)
        def _(kt):
            keys = rows_of(kt)
            probs = p_buf[kt] * inverse
            ds = (probs * (g_buf[kt] - dot_row)).astype(jnp.bfloat16)
            dv_acc[keys, :] += lax.dot_general(
                probs.astype(jnp.bfloat16), o_tile, NN, preferred_element_type=f32
            )
            dk_acc[keys, :] += lax.dot_general(ds, q_tile, NN, preferred_element_type=f32)
            dq_acc[...] += lax.dot_general(k_turn[:, keys], ds, NN, preferred_element_type=f32)

        dq_ref[mine, :] = (dq_acc[...] * SCALE).T.astype(jnp.bfloat16)

    @pl.loop(0, TOTAL // KT)
    def _(kt):
        keys = pl.ds(pl.multiple_of(kt * KT, KT), KT)
        dk_ref[keys, :] = (dk_acc[keys, :] * SCALE).astype(jnp.bfloat16)
        dv_ref[keys, :] = dv_acc[keys, :].astype(jnp.bfloat16)


def attention_call(docs, q, o, k, v):
    vm = pl.BlockSpec(memory_space=pltpu.VMEM)
    bf, f32 = jnp.bfloat16, jnp.float32
    tiles = TOTAL // KT
    return pl.pallas_call(
        attention_kernel,
        out_shape=(
            jax.ShapeDtypeStruct((QLOCAL, HD), bf),
            jax.ShapeDtypeStruct((TOTAL, HD), bf),
            jax.ShapeDtypeStruct((TOTAL, HD), bf),
        ),
        in_specs=[vm] * 5,
        out_specs=(vm, vm, vm),
        scratch_shapes=[
            pltpu.VMEM((tiles, KT, QT), f32),
            pltpu.VMEM((tiles, KT, QT), f32),
            pltpu.VMEM((TOTAL, HD), f32),
            pltpu.VMEM((TOTAL, HD), f32),
            pltpu.VMEM((HD, QT), f32),
            pltpu.VMEM((HD, TOTAL), bf),
        ],
        compiler_params=pltpu.CompilerParams(
            vmem_limit_bytes=32 << 20
        ),
        name="attention_grads",
    )(docs, q, o, k, v)


def return_kernel(
    dq_ref, dk_ref, dv_ref,
    qo, ko, vo,
    sib_buf, x_buf, stage,
    q_send, q_recv, sib_send, sib_recv, x_send, x_recv, y_send, y_recv,
):
    s, g, x, y, k = place()
    sibling = seq_of(x, y, 1 - k)
    other = seq_of(1 - x, y, k)
    barrier_with([((s + i) % 16, g) for i in range(1, 16)])
    parts = (dk_ref, dv_ref)
    outs = (ko, vo)
    order = (2, 1, 3, 0)

    def column(n):
        return 1 - x if n < 4 else x

    def sib_copy(n, i):
        src = parts[i].at[block_rows(seq_of(column(n), (y + n) % 4, 1 - k))]
        return remote(src, sib_buf.at[n, i], sib_send.at[n, i], sib_recv.at[n, i], sibling, g)

    def x_copy(dy, i):
        return remote(stage.at[dy, i], x_buf.at[dy, i], x_send.at[dy, i], x_recv.at[dy, i], other, g)

    def y_copy(dy, i):
        return remote(
            stage.at[4 + dy, i], outs[i].at[:, head_cols(y)], y_send.at[dy, i], y_recv.at[dy, i],
            seq_of(x, (y + dy) % 4, k), g,
        )

    @pl.when(x == 1)
    def _():
        for dy in order:
            for i in range(2):
                sib_copy(dy, i).start()

    def q_piece(n):
        tile = tile_of(x, k, n // 2)
        chip, u = tile // 3, (tile % 3) * 2 + n % 2
        tk, j = u // 3, u % 3
        src = dq_ref.at[pl.ds(n * HD, HD)]
        dst = qo.at[pl.ds(pl.multiple_of(j * HD, HD), HD), head_cols(y)]
        return chip * 2 + tk, j, src, dst

    for n in range(12):
        to, j, src, dst = q_piece(n)

        @pl.when(to == s)
        def _():
            pltpu.make_async_copy(src, dst, q_recv.at[y, j]).start()

        @pl.when(to != s)
        def _():
            remote(src, dst, q_send.at[n], q_recv.at[y, j], to, g).start()

    for dy in order:
        for i in range(2):
            sib_copy(4 + dy, i).start()

    def summed(n, i, extra):
        sib_copy(n, i).wait_recv()
        rows = block_rows(seq_of(column(n), (y + n) % 4, k))
        total = parts[i][rows, :].astype(jnp.float32) + sib_buf[n, i].astype(jnp.float32)
        if extra:
            x_copy(n - 4, i).wait_recv()
            total = total + x_buf[n - 4, i].astype(jnp.float32)
        stage[n, i] = total.astype(jnp.bfloat16)

    def own_column(extra):
        for dy in order:
            for i in range(2):
                summed(4 + dy, i, extra)
                if dy:
                    y_copy(dy, i).start()
                else:
                    pltpu.make_async_copy(
                        stage.at[4, i], outs[i].at[:, head_cols(y)], y_recv.at[0, i]
                    ).start()

    @pl.when(x == 1)
    def _():
        for dy in order:
            for i in range(2):
                summed(dy, i, False)
                x_copy(dy, i).start()
        own_column(False)

    @pl.when(x == 0)
    def _():
        own_column(True)

    for ty in range(4):
        for j in range(3):
            dst = qo.at[pl.ds(j * HD, HD), pl.ds(ty * HD, HD)]
            pltpu.make_async_copy(dst, dst, q_recv.at[ty, j]).wait()
    for n in range(12):
        to, j, src, dst = q_piece(n)

        @pl.when(to != s)
        def _():
            remote(src, dst, q_send.at[n], q_recv.at[y, j], to, g).wait_send()
    for dy in range(4):
        for i in range(2):
            dst = outs[i].at[:, head_cols((y + 4 - dy) % 4)]
            pltpu.make_async_copy(dst, dst, y_recv.at[dy, i]).wait()
            sib_copy(4 + dy, i).wait_send()
            if dy:
                y_copy(dy, i).wait_send()

    @pl.when(x == 1)
    def _():
        for dy in range(4):
            for i in range(2):
                sib_copy(dy, i).wait_send()
                x_copy(dy, i).wait_send()


def return_call(dq, dk, dv):
    vm = pl.BlockSpec(memory_space=pltpu.VMEM)
    anyspace = pl.BlockSpec(memory_space=pl.ANY)
    dma = pltpu.SemaphoreType.DMA
    bf = jnp.bfloat16
    return pl.pallas_call(
        return_kernel,
        out_shape=(jax.ShapeDtypeStruct((ROWS, COLS), bf),) * 3,
        in_specs=[vm, vm, vm],
        out_specs=(anyspace,) * 3,
        scratch_shapes=[
            pltpu.VMEM((8, 2, ROWS, HD), bf),
            pltpu.VMEM((4, 2, ROWS, HD), bf),
            pltpu.VMEM((8, 2, ROWS, HD), bf),
            dma((12,)), dma((4, 3)), dma((8, 2)), dma((8, 2)),
            dma((4, 2)), dma((4, 2)), dma((4, 2)), dma((4, 2)),
        ],
        compiler_params=pltpu.CompilerParams(
            collective_id=1, has_side_effects=True, vmem_limit_bytes=8 << 20
        ),
        name="return_grads",
    )(dq, dk, dv)


def store_kernel(a, b, c, ao, bo, co, sem):
    copies = [
        pltpu.make_async_copy(src, dst, sem.at[i])
        for i, (src, dst) in enumerate(((a, ao), (b, bo), (c, co)))
    ]
    for copy in copies:
        copy.start()
    for copy in copies:
        copy.wait()


def store_call(*arrays):
    vm = pl.BlockSpec(memory_space=pltpu.VMEM)
    hbm = pl.BlockSpec(memory_space=pltpu.HBM)
    return pl.pallas_call(
        store_kernel,
        out_shape=(jax.ShapeDtypeStruct((ROWS, COLS), jnp.bfloat16),) * 3,
        in_specs=[vm] * 3,
        out_specs=(hbm,) * 3,
        scratch_shapes=[pltpu.SemaphoreType.DMA((3,))],
        compiler_params=pltpu.CompilerParams(vmem_limit_bytes=4 << 20),
        name="store_grads",
    )(*arrays)


def per_device(queries, keys_in, values, out_grad, out_weight, doc_ids):
    k, v, q, o, docs = gather_call(
        queries, keys_in, values, out_grad, out_weight, doc_ids.reshape(3, HD)
    )
    dq, dk, dv = attention_call(docs, q, o, k, v)
    return store_call(*return_call(dq, dk, dv))


def solution(mesh):
    in_specs = (
        P("seq", "head"),
        P("seq", "head"),
        P("seq", "head"),
        P("seq", "head"),
        P("head", None),
        P("seq"),
    )
    out_specs = (P("seq", "head"), P("seq", "head"), P("seq", "head"))
    return jax.shard_map(
        per_device, mesh=mesh, in_specs=in_specs, out_specs=out_specs, check_vma=False
    )
```

```python
import functools

import jax
import jax.numpy as jnp
from jax import lax
from jax.experimental import pallas as pl
from jax.experimental.pallas import tpu as pltpu
from jax.sharding import PartitionSpec as P

HD = 128
ROWS = 384
COLS = 512
HEADS_LOCAL = 4
TOTAL = 6144
QT = 256
KT = 512
QLOCAL = 1536
NCH = 6
CH = ROWS // NCH
NEG = -1e30
SCALE = HD ** -0.5
LOG2E = 1.4426950408889634
MESH = pl.DeviceIdType.MESH
NT = (((1,), (1,)), ((), ()))
TN = (((0,), (0,)), ((), ()))
NN = (((1,), (0,)), ((), ()))


def place():
    s = lax.axis_index("seq")
    g = lax.axis_index("head")
    x = s // 8
    y = (s // 2) % 4
    k = s % 2
    return s, g, x, y, k


def seq_of(x, y, k):
    return (x * 4 + y) * 2 + k


def remote(src, dst, send, recv, seq, head):
    return pltpu.make_async_remote_copy(
        src_ref=src,
        dst_ref=dst,
        send_sem=send,
        recv_sem=recv,
        device_id={"seq": seq, "head": head},
        device_id_type=MESH,
    )


def barrier_with(peers):
    barrier = pltpu.get_barrier_semaphore()
    for seq, head in peers:
        pl.semaphore_signal(
            barrier, inc=1, device_id={"seq": seq, "head": head}, device_id_type=MESH
        )
    pl.semaphore_wait(barrier, len(peers))


def block_rows(s):
    return pl.ds(pl.multiple_of(s * ROWS, 128), ROWS)


def head_cols(y):
    return pl.ds(pl.multiple_of(y * HD, HD), HD)


def slot_of(y, k, j):
    u = 3 * k + j
    return u % 2, 3 * y + u // 2


def gather_kernel(
    q_ref, k_ref, v_ref, og_hbm, w_hbm, doc_ref,
    ko, vo, qo, do, doco,
    land, w_ref, acc, grad,
    g_send, g_recv, y_send, y_recv, sib_send, sib_recv, x_send, x_recv,
    q_send, q_recv, o_send, o_recv, d_send, d_recv, w_sem, l_sem,
):
    s, g, x, y, k = place()
    xh, z = g // 4, g % 4
    up = xh * 4 + (z + 1) % 4
    down = xh * 4 + (z + 3) % 4
    across = (1 - xh) * 4 + z
    sibling = seq_of(x, y, 1 - k)
    other = seq_of(1 - x, y, k)

    og_copy = pltpu.make_async_copy(og_hbm, land.at[0], g_recv.at[0, 0])
    og_copy.start()
    w_copy = pltpu.make_async_copy(w_hbm, w_ref, w_sem)
    w_copy.start()
    barrier_with(
        [((s + i) % 16, g) for i in range(1, 16)] + [(s, up), (s, down), (s, across)]
    )

    sends = []

    def go(copy):
        copy.start()
        sends.append(copy)

    def rows(c):
        return pl.ds(c * CH, CH)

    order = ((0, 5), (1, 4), (2, 3), (3, 2), (4, 1), (5, 0))

    def ring(n, src, slot, c, head):
        return remote(src, land.at[slot, rows(c)], g_send.at[n, c], g_recv.at[slot, c], s, head)

    for (up_c, down_c), across_c in zip(order, (0, 5, 1, 4, 2, 3)):
        go(ring(0, og_hbm.at[rows(up_c)], 1, up_c, up))
        go(ring(1, og_hbm.at[rows(down_c)], 2, down_c, down))
        go(ring(2, og_hbm.at[rows(across_c)], 4, across_c, across))

    mine = block_rows(s)
    local = []
    for i, (src, dst) in enumerate(((k_ref, ko), (v_ref, vo))):
        copy = pltpu.make_async_copy(src.at[:, head_cols(y)], dst.at[mine], l_sem.at[i])
        copy.start()
        local.append(copy)
    for dy in (2, 1, 3):
        ty = (y + dy) % 4
        for i, (src, dst) in enumerate(((k_ref, ko), (v_ref, vo))):
            go(remote(src.at[:, head_cols(ty)], dst.at[mine], y_send.at[dy, i],
                      y_recv.at[dy, i], seq_of(x, ty, k), g))

    def x_copy(src, dst, where, dy, i):
        return remote(src, dst.at[where], x_send.at[dy, i], x_recv.at[dy, i], other, g)

    def sib_copy(src, dst, where, n, i):
        return remote(src, dst.at[where], sib_send.at[n, i], sib_recv.at[n, i], sibling, g)

    for i, (src, dst) in enumerate(((k_ref, ko), (v_ref, vo))):
        go(sib_copy(src.at[:, head_cols(y)], dst, mine, 0, i))


    def spread(src, dst, send, recv, pieces=(0, 2, 1)):
        for dy in (2, 1, 3, 0):
            ty = (y + dy) % 4
            for j in pieces:
                core, slot = slot_of(y, k, j)
                piece = src.at[pl.ds(j * HD, HD), head_cols(ty)]
                there = dst.at[pl.ds(pl.multiple_of(slot * HD, HD), HD)]
                if dy:
                    go(remote(piece, there, send.at[dy, j], recv.at[slot], seq_of(x, ty, core), g))
                else:
                    @pl.when(core != k)
                    def _():
                        remote(piece, there, send.at[0, j], recv.at[slot],
                               sibling, g).start()

                    @pl.when(core == k)
                    def _():
                        pltpu.make_async_copy(piece, there, recv.at[slot]).start()

    def drain(src, dst, send, recv):
        for j in range(3):
            core, slot = slot_of(y, k, j)
            piece = src.at[pl.ds(j * HD, HD), head_cols(y)]
            there = dst.at[pl.ds(pl.multiple_of(slot * HD, HD), HD)]

            @pl.when(core != k)
            def _():
                remote(piece, there, send.at[0, j], recv.at[slot],
                       sibling, g).wait_send()
        for slot in range(12):
            there = dst.at[pl.ds(slot * HD, HD)]
            pltpu.make_async_copy(there, there, recv.at[slot]).wait()

    for i in range(1, 16):
        go(remote(doc_ref, doco.at[s], d_send.at[i], d_recv.at[i], (s + i) % 16, g))
    own_doc = pltpu.make_async_copy(doc_ref, doco.at[s], d_recv.at[0])
    own_doc.start()

    def got(slot, c):
        ring(0, land.at[slot, rows(c)], slot, c, up).wait_recv()

    def relay_kv(dy):
        where = block_rows(seq_of(x, (y + 4 - dy) % 4, k))
        for i, dst in enumerate((ko, vo)):
            remote(dst.at[where], dst.at[where], y_send.at[dy, i], y_recv.at[dy, i], sibling, g).wait_recv()
            go(sib_copy(dst.at[where], dst, where, dy, i))

    def from_x(dy):
        where = block_rows(seq_of(0, (y + 4 - dy) % 4, k))

        @pl.when(x == 1)
        def _():
            for i, dst in enumerate((ko, vo)):
                x_copy(dst.at[where], dst, where, dy, i).wait_recv()
                sib_copy(dst.at[where], dst, where, 4 + dy, i).start()

    def pass_on(slot):
        for c, e in order[:3]:
            got(slot, c)
            go(ring(slot + 2, land.at[slot, rows(c)], slot + 2, c, up))
            got(slot + 1, e)
            go(ring(slot + 2, land.at[slot + 1, rows(e)], slot + 2, e, down))

    def share(c):
        got(4, c)
        go(ring(4, land.at[4, rows(c)], 5, c, up))
        go(ring(5, land.at[4, rows(c)], 6, c, down))

    pass_on(1)
    share(0)
    relay_kv(1)
    share(5)
    relay_kv(3)
    share(1)
    share(4)
    relay_kv(2)
    share(2)
    share(3)
    @pl.when(x == 0)
    def _():
        for i, (src, dst) in enumerate(((k_ref, ko), (v_ref, vo))):
            x_copy(src.at[:, head_cols(y)], dst, mine, 0, i).start()
        for dy in (1, 3, 2):
            where = block_rows(seq_of(0, (y + 4 - dy) % 4, k))
            for i, dst in enumerate((ko, vo)):
                x_copy(dst.at[where], dst, where, dy, i).start()
    spread(q_ref, qo, q_send, q_recv)

    w_copy.wait()

    def product(slot, head):
        block = land[slot]
        weights = w_ref[:, pl.ds(pl.multiple_of(head * COLS, COLS), COLS)]
        part = lax.dot_general(block, weights, NT, preferred_element_type=jnp.float32)
        acc[...] = part if slot == 0 else acc[...] + part

    far = xh * 4 + (z + 2) % 4
    turn = (1 - xh) * 4
    og_copy.wait()
    product(0, g)
    for c, e in order[:3]:
        got(1, e)
        got(2, c)
    product(1, down)
    product(2, up)
    from_x(0)
    for c, e in order[:3]:
        got(3, c)
        got(3, e)
    product(3, far)
    product(4, across)
    pass_on(5)
    from_x(1)
    for c, e in order[:3]:
        got(5, e)
        got(6, c)
    product(5, turn + (z + 3) % 4)
    product(6, turn + (z + 1) % 4)
    from_x(3)

    last = turn + (z + 2) % 4
    weights = w_ref[:, pl.ds(pl.multiple_of(last * COLS, COLS), COLS)]

    def finish(j):
        piece = pl.ds(j * HD, HD)
        part = lax.dot_general(land[7, piece], weights, NT, preferred_element_type=jnp.float32)
        grad[piece] = (acc[piece] + part).astype(jnp.bfloat16)
        spread(grad, do, o_send, o_recv, (j,))

    for c, e in order[:2]:
        got(7, c)
        got(7, e)
    finish(0)
    finish(2)
    for c in (2, 3):
        got(7, c)
    finish(1)
    from_x(2)

    for copy in local:
        copy.wait()
    own_doc.wait()
    for i in range(1, 16):
        remote(doc_ref, doco.at[(s + 16 - i) % 16], d_send.at[i], d_recv.at[i], s, g).wait_recv()
    for dy in range(4):
        where = block_rows(seq_of(x, (y + 4 - dy) % 4, 1 - k))
        for i, dst in enumerate((ko, vo)):
            sib_copy(dst.at[where], dst, where, dy, i).wait_recv()

    @pl.when(x == 0)
    def _():
        for dy in range(4):
            where = block_rows(seq_of(0, (y + 4 - dy) % 4, k))
            for i, dst in enumerate((ko, vo)):
                x_copy(dst.at[where], dst, where, dy, i).wait_send()

    @pl.when(x == 1)
    def _():
        for dy in range(4):
            where = block_rows(seq_of(0, (y + 4 - dy) % 4, 1 - k))
            for i, dst in enumerate((ko, vo)):
                copy = sib_copy(dst.at[where], dst, where, 4 + dy, i)
                copy.wait_recv()
                copy.wait_send()
    drain(q_ref, qo, q_send, q_recv)
    drain(grad, do, o_send, o_recv)
    for copy in sends:
        copy.wait_send()


def gather_call(queries, keys_in, values, out_grad, out_weight, docs):
    hbm = pl.BlockSpec(memory_space=pltpu.HBM)
    anyspace = pl.BlockSpec(memory_space=pl.ANY)
    dma = pltpu.SemaphoreType.DMA
    bf = jnp.bfloat16
    return pl.pallas_call(
        gather_kernel,
        out_shape=(
            jax.ShapeDtypeStruct((TOTAL, HD), bf),
            jax.ShapeDtypeStruct((TOTAL, HD), bf),
            jax.ShapeDtypeStruct((QLOCAL, HD), bf),
            jax.ShapeDtypeStruct((QLOCAL, HD), bf),
            jax.ShapeDtypeStruct((16, 3, HD), jnp.int32),
        ),
        in_specs=[hbm] * 6,
        out_specs=(anyspace,) * 5,
        scratch_shapes=[
            pltpu.VMEM((8, ROWS, COLS), bf),
            pltpu.VMEM((COLS, 4096), bf),
            pltpu.VMEM((ROWS, COLS), jnp.float32),
            pltpu.VMEM((ROWS, COLS), bf),
            dma((8, NCH)), dma((8, NCH)), dma((4, 2)), dma((4, 2)),
            dma((8, 2)), dma((8, 2)), dma((4, 2)), dma((4, 2)),
            dma((4, 3)), dma((12,)), dma((4, 3)), dma((12,)),
            dma((16,)), dma((16,)), dma, dma((2,)),
        ],
        compiler_params=pltpu.CompilerParams(
            collective_id=0, has_side_effects=True, vmem_limit_bytes=12 << 20
        ),
        name="spread_rows",
    )(
        *(
            pltpu.with_memory_space_constraint(a, pltpu.HBM)
            for a in (queries, keys_in, values, out_grad, out_weight, docs)
        )
    )


def attention_kernel(
    doc_v, q_ref, o_ref, k_ref, v_ref,
    dq_ref, dk_ref, dv_ref,
    p_buf, g_buf, dk_acc, dv_acc, dq_acc,
):
    s, g, x, y, k = place()
    docs = doc_v[...]
    starts = [jnp.int32(0)]
    for d in range(1, 8):
        starts.append(jnp.sum(jnp.where(docs < d, 1, 0)))
    dk_acc[...] = jnp.zeros_like(dk_acc)
    dv_acc[...] = jnp.zeros_like(dv_acc)
    factor = SCALE * LOG2E
    lane = lax.broadcasted_iota(jnp.int32, (1, QT), 1)
    sub = lax.broadcasted_iota(jnp.int32, (KT, QT), 0)
    f32 = jnp.float32

    def folded(value, reduce):
        return reduce(value.reshape(KT // 8, 8, QT), axis=0)

    @pl.loop(0, QLOCAL // QT)
    def _(t):
        diagonal = 6 * x + t
        unit = 4 * diagonal + k
        mine = pl.ds(pl.multiple_of(t * QT, QT), QT)
        q_tile = q_ref[mine, :]
        o_tile = o_ref[mine, :]
        doc_q = jnp.concatenate(
            [doc_v[u // 3, pl.ds(u % 3, 1), :] for u in (unit, unit + 2)], axis=1
        )
        start = jnp.zeros((1, QT), jnp.int32)
        for d in range(1, 8):
            start = jnp.where(doc_q == d, starts[d], start)
        k_low = jnp.min(start) // KT
        k_full = jnp.minimum((jnp.max(start) + KT - 1) // KT, diagonal)
        pos = unit * HD + lane + jnp.where(lane >= HD, HD, 0)

        def rows_of(kt):
            return pl.ds(pl.multiple_of(kt * KT, KT), KT)

        def plain(kt, top):
            scores = lax.dot_general(k_ref[rows_of(kt), :], q_tile, NT, preferred_element_type=f32)
            p_buf[kt] = scores
            return jnp.maximum(top, folded(scores, jnp.max))

        def masked(kt, top):
            scores = lax.dot_general(k_ref[rows_of(kt), :], q_tile, NT, preferred_element_type=f32)
            key = kt * KT + sub
            scores = jnp.where((key >= start) & (key <= pos), scores, NEG)
            p_buf[kt] = scores
            return jnp.maximum(top, folded(scores, jnp.max))

        top = jnp.full((8, QT), NEG, f32)
        top = lax.fori_loop(k_low, k_full, masked, top)
        top = lax.fori_loop(k_full, diagonal, plain, top)
        top = jnp.max(masked(diagonal, top), axis=0, keepdims=True)

        def weigh(kt, carry):
            total, weighted = carry
            p = jnp.exp2((p_buf[kt] - top) * factor)
            gp = lax.dot_general(v_ref[rows_of(kt), :], o_tile, NT, preferred_element_type=f32)
            p_buf[kt] = p
            g_buf[kt] = gp
            return total + folded(p, jnp.sum), weighted + folded(p * gp, jnp.sum)

        zero = jnp.zeros((8, QT), f32)
        total, weighted = lax.fori_loop(k_low, diagonal + 1, weigh, (zero, zero))
        inverse = 1.0 / jnp.sum(total, axis=0, keepdims=True)
        dot_row = jnp.sum(weighted, axis=0, keepdims=True) * inverse
        dq_acc[...] = jnp.zeros_like(dq_acc)

        @pl.loop(k_low, diagonal + 1)
        def _(kt):
            keys = rows_of(kt)
            probs = p_buf[kt] * inverse
            ds = (probs * (g_buf[kt] - dot_row)).astype(jnp.bfloat16)
            dv_acc[keys, :] += lax.dot_general(
                probs.astype(jnp.bfloat16), o_tile, NN, preferred_element_type=f32
            )
            dk_acc[keys, :] += lax.dot_general(ds, q_tile, NN, preferred_element_type=f32)
            dq_acc[...] += lax.dot_general(k_ref[keys, :], ds, TN, preferred_element_type=f32)

        dq_ref[mine, :] = (dq_acc[...] * SCALE).T.astype(jnp.bfloat16)

    @pl.loop(0, TOTAL // KT)
    def _(kt):
        keys = pl.ds(pl.multiple_of(kt * KT, KT), KT)
        dk_ref[keys, :] = (dk_acc[keys, :] * SCALE).astype(jnp.bfloat16)
        dv_ref[keys, :] = dv_acc[keys, :].astype(jnp.bfloat16)


def attention_call(docs, q, o, k, v):
    vm = pl.BlockSpec(memory_space=pltpu.VMEM)
    bf, f32 = jnp.bfloat16, jnp.float32
    tiles = TOTAL // KT
    return pl.pallas_call(
        attention_kernel,
        out_shape=(
            jax.ShapeDtypeStruct((QLOCAL, HD), bf),
            jax.ShapeDtypeStruct((TOTAL, HD), bf),
            jax.ShapeDtypeStruct((TOTAL, HD), bf),
        ),
        in_specs=[vm] * 5,
        out_specs=(vm, vm, vm),
        scratch_shapes=[
            pltpu.VMEM((tiles, KT, QT), f32),
            pltpu.VMEM((tiles, KT, QT), f32),
            pltpu.VMEM((TOTAL, HD), f32),
            pltpu.VMEM((TOTAL, HD), f32),
            pltpu.VMEM((HD, QT), f32),
        ],
        compiler_params=pltpu.CompilerParams(
            vmem_limit_bytes=32 << 20
        ),
        name="attention_grads",
    )(docs, q, o, k, v)


def return_kernel(
    dq_ref, dk_ref, dv_ref,
    qo, ko, vo,
    sib_buf, x_buf, pass_buf, stage,
    q_send, q_recv, sib_send, sib_recv, x_send, x_recv, y_send, y_recv, p_send, p_recv,
):
    s, g, x, y, k = place()
    beyond = (1 - g // 4) * 4 + g % 4
    sibling = seq_of(x, y, 1 - k)
    other = seq_of(1 - x, y, k)
    barrier_with([((s + i) % 16, g) for i in range(1, 16)] + [(other, beyond)])
    parts = (dk_ref, dv_ref)
    outs = (ko, vo)
    order = (2, 1, 3, 0)
    late = (1, 3, 2, 0)

    def column(n):
        return 1 - x if n < 4 else x

    def sib_copy(n, i):
        src = parts[i].at[block_rows(seq_of(column(n), (y + n) % 4, 1 - k))]
        return remote(src, sib_buf.at[n, i], sib_send.at[n, i], sib_recv.at[n, i], sibling, g)

    def x_copy(dy, i):
        return remote(stage.at[dy, i], x_buf.at[dy, i], x_send.at[dy, i], x_recv.at[dy, i], other, g)

    def first_leg(i):
        return remote(stage.at[2, i], pass_buf.at[i], p_send.at[i], p_recv.at[i], other, beyond)

    def second_leg(i):
        return remote(pass_buf.at[i], pass_buf.at[i], p_send.at[i], p_recv.at[i], other, g)

    def third_leg(i):
        return remote(pass_buf.at[i], x_buf.at[2, i], x_send.at[2, i], x_recv.at[2, i], other, beyond)

    def y_copy(dy, i):
        return remote(
            stage.at[4 + dy, i], outs[i].at[:, head_cols(y)], y_send.at[dy, i], y_recv.at[dy, i],
            seq_of(x, (y + dy) % 4, k), g,
        )

    @pl.when(x == 1)
    def _():
        for dy in order:
            for i in range(2):
                sib_copy(dy, i).start()

    def q_piece(n):
        chip, u = 4 * x + n // 3, (n % 3) * 2 + k
        tk, j = u // 3, u % 3
        src = dq_ref.at[pl.ds(n * HD, HD)]
        dst = qo.at[pl.ds(pl.multiple_of(j * HD, HD), HD), head_cols(y)]
        return chip * 2 + tk, j, src, dst

    for n in range(12):
        to, j, src, dst = q_piece(n)

        @pl.when(to == s)
        def _():
            pltpu.make_async_copy(src, dst, q_recv.at[y, j]).start()

        @pl.when(to != s)
        def _():
            remote(src, dst, q_send.at[n], q_recv.at[y, j], to, g).start()

    for dy in order:
        for i in range(2):
            sib_copy(4 + dy, i).start()

    def summed(n, i, extra):
        sib_copy(n, i).wait_recv()
        rows = block_rows(seq_of(column(n), (y + n) % 4, k))
        total = parts[i][rows, :].astype(jnp.float32) + sib_buf[n, i].astype(jnp.float32)
        if extra:
            x_copy(n - 4, i).wait_recv()
            total = total + x_buf[n - 4, i].astype(jnp.float32)
        stage[n, i] = total.astype(jnp.bfloat16)

    def own_column(extra):
        for dy in late:
            for i in range(2):
                summed(4 + dy, i, extra)
                if dy:
                    y_copy(dy, i).start()
                else:
                    pltpu.make_async_copy(
                        stage.at[4, i], outs[i].at[:, head_cols(y)], y_recv.at[0, i]
                    ).start()

    @pl.when(x == 1)
    def _():
        for dy in order:
            for i in range(2):
                summed(dy, i, False)
                if dy == 2:
                    first_leg(i).start()
                else:
                    x_copy(dy, i).start()
        for i in range(2):
            second_leg(i).wait_recv()
            third_leg(i).start()
        own_column(False)

    @pl.when(x == 0)
    def _():
        for i in range(2):
            first_leg(i).wait_recv()
            second_leg(i).start()
        own_column(True)
        for i in range(2):
            second_leg(i).wait_send()

    for ty in range(4):
        for j in range(3):
            dst = qo.at[pl.ds(j * HD, HD), pl.ds(ty * HD, HD)]
            pltpu.make_async_copy(dst, dst, q_recv.at[ty, j]).wait()
    for n in range(12):
        to, j, src, dst = q_piece(n)

        @pl.when(to != s)
        def _():
            remote(src, dst, q_send.at[n], q_recv.at[y, j], to, g).wait_send()
    for dy in range(4):
        for i in range(2):
            dst = outs[i].at[:, head_cols((y + 4 - dy) % 4)]
            pltpu.make_async_copy(dst, dst, y_recv.at[dy, i]).wait()
            sib_copy(4 + dy, i).wait_send()
            if dy:
                y_copy(dy, i).wait_send()

    @pl.when(x == 1)
    def _():
        for dy in range(4):
            for i in range(2):
                sib_copy(dy, i).wait_send()
                if dy == 2:
                    first_leg(i).wait_send()
                    third_leg(i).wait_send()
                else:
                    x_copy(dy, i).wait_send()


def return_call(dq, dk, dv):
    vm = pl.BlockSpec(memory_space=pltpu.VMEM)
    anyspace = pl.BlockSpec(memory_space=pl.ANY)
    dma = pltpu.SemaphoreType.DMA
    bf = jnp.bfloat16
    return pl.pallas_call(
        return_kernel,
        out_shape=(jax.ShapeDtypeStruct((ROWS, COLS), bf),) * 3,
        in_specs=[vm, vm, vm],
        out_specs=(anyspace,) * 3,
        scratch_shapes=[
            pltpu.VMEM((8, 2, ROWS, HD), bf),
            pltpu.VMEM((4, 2, ROWS, HD), bf),
            pltpu.VMEM((2, ROWS, HD), bf),
            pltpu.VMEM((8, 2, ROWS, HD), bf),
            dma((12,)), dma((4, 3)), dma((8, 2)), dma((8, 2)),
            dma((4, 2)), dma((4, 2)), dma((4, 2)), dma((4, 2)), dma((2,)), dma((2,)),
        ],
        compiler_params=pltpu.CompilerParams(
            collective_id=1, has_side_effects=True, vmem_limit_bytes=8 << 20
        ),
        name="return_grads",
    )(dq, dk, dv)


def store_kernel(a, b, c, ao, bo, co, sem):
    copies = [
        pltpu.make_async_copy(src, dst, sem.at[i])
        for i, (src, dst) in enumerate(((a, ao), (b, bo), (c, co)))
    ]
    for copy in copies:
        copy.start()
    for copy in copies:
        copy.wait()


def store_call(*arrays):
    vm = pl.BlockSpec(memory_space=pltpu.VMEM)
    hbm = pl.BlockSpec(memory_space=pltpu.HBM)
    return pl.pallas_call(
        store_kernel,
        out_shape=(jax.ShapeDtypeStruct((ROWS, COLS), jnp.bfloat16),) * 3,
        in_specs=[vm] * 3,
        out_specs=(hbm,) * 3,
        scratch_shapes=[pltpu.SemaphoreType.DMA((3,))],
        compiler_params=pltpu.CompilerParams(vmem_limit_bytes=4 << 20),
        name="store_grads",
    )(*arrays)


def per_device(queries, keys_in, values, out_grad, out_weight, doc_ids):
    k, v, q, o, docs = gather_call(
        queries, keys_in, values, out_grad, out_weight, doc_ids.reshape(3, HD)
    )
    dq, dk, dv = attention_call(docs, q, o, k, v)
    return store_call(*return_call(dq, dk, dv))


def solution(mesh):
    in_specs = (
        P("seq", "head"),
        P("seq", "head"),
        P("seq", "head"),
        P("seq", "head"),
        P("head", None),
        P("seq"),
    )
    out_specs = (P("seq", "head"), P("seq", "head"), P("seq", "head"))
    return jax.shard_map(
        per_device, mesh=mesh, in_specs=in_specs, out_specs=out_specs, check_vma=False
    )
```

```python
import functools

import jax
import jax.numpy as jnp
from jax import lax
from jax.experimental import pallas as pl
from jax.experimental.pallas import tpu as pltpu
from jax.sharding import PartitionSpec as P

HD = 128
ROWS = 384
COLS = 512
HEADS_LOCAL = 4
TOTAL = 6144
QT = 256
KT = 512
QLOCAL = 1536
NCH = 6
CH = ROWS // NCH
NEG = -1e30
SCALE = HD ** -0.5
LOG2E = 1.4426950408889634
MESH = pl.DeviceIdType.MESH
NT = (((1,), (1,)), ((), ()))
TN = (((0,), (0,)), ((), ()))
NN = (((1,), (0,)), ((), ()))


def place():
    s = lax.axis_index("seq")
    g = lax.axis_index("head")
    x = s // 8
    y = (s // 2) % 4
    k = s % 2
    return s, g, x, y, k


def seq_of(x, y, k):
    return (x * 4 + y) * 2 + k


def remote(src, dst, send, recv, seq, head):
    return pltpu.make_async_remote_copy(
        src_ref=src,
        dst_ref=dst,
        send_sem=send,
        recv_sem=recv,
        device_id={"seq": seq, "head": head},
        device_id_type=MESH,
    )


def barrier_with(peers):
    barrier = pltpu.get_barrier_semaphore()
    for seq, head in peers:
        pl.semaphore_signal(
            barrier, inc=1, device_id={"seq": seq, "head": head}, device_id_type=MESH
        )
    pl.semaphore_wait(barrier, len(peers))


def block_rows(s):
    return pl.ds(pl.multiple_of(s * ROWS, 128), ROWS)


def head_cols(y):
    return pl.ds(pl.multiple_of(y * HD, HD), HD)


def slot_of(y, k, j):
    u = 3 * k + j
    return u % 2, 3 * y + u // 2


def gather_kernel(
    q_ref, k_ref, v_ref, og_hbm, w_hbm, doc_ref,
    ko, vo, qo, do, doco,
    land, w_ref, acc, grad,
    g_send, g_recv, y_send, y_recv, sib_send, sib_recv, x_send, x_recv,
    q_send, q_recv, o_send, o_recv, d_send, d_recv, w_sem, l_sem,
):
    s, g, x, y, k = place()
    xh, z = g // 4, g % 4
    up = xh * 4 + (z + 1) % 4
    down = xh * 4 + (z + 3) % 4
    across = (1 - xh) * 4 + z
    sibling = seq_of(x, y, 1 - k)
    other = seq_of(1 - x, y, k)

    og_copy = pltpu.make_async_copy(og_hbm, land.at[0], g_recv.at[0, 0])
    og_copy.start()
    w_copy = pltpu.make_async_copy(w_hbm, w_ref, w_sem)
    w_copy.start()
    barrier_with(
        [((s + i) % 16, g) for i in range(1, 16)] + [(s, up), (s, down), (s, across)]
    )

    sends = []

    def go(copy):
        copy.start()
        sends.append(copy)

    def rows(c):
        return pl.ds(c * CH, CH)

    order = ((0, 5), (1, 4), (2, 3), (3, 2), (4, 1), (5, 0))

    def ring(n, src, slot, c, head):
        return remote(src, land.at[slot, rows(c)], g_send.at[n, c], g_recv.at[slot, c], s, head)

    for (up_c, down_c), across_c in zip(order, (0, 5, 1, 4, 2, 3)):
        go(ring(0, og_hbm.at[rows(up_c)], 1, up_c, up))
        go(ring(1, og_hbm.at[rows(down_c)], 2, down_c, down))
        go(ring(2, og_hbm.at[rows(across_c)], 4, across_c, across))

    mine = block_rows(s)
    local = []
    for i, (src, dst) in enumerate(((k_ref, ko), (v_ref, vo))):
        copy = pltpu.make_async_copy(src.at[:, head_cols(y)], dst.at[mine], l_sem.at[i])
        copy.start()
        local.append(copy)
    for dy in (2, 1, 3):
        ty = (y + dy) % 4
        for i, (src, dst) in enumerate(((k_ref, ko), (v_ref, vo))):
            go(remote(src.at[:, head_cols(ty)], dst.at[mine], y_send.at[dy, i],
                      y_recv.at[dy, i], seq_of(x, ty, k), g))

    def x_copy(src, dst, where, dy, i):
        return remote(src, dst.at[where], x_send.at[dy, i], x_recv.at[dy, i], other, g)

    def sib_copy(src, dst, where, n, i):
        return remote(src, dst.at[where], sib_send.at[n, i], sib_recv.at[n, i], sibling, g)

    for i, (src, dst) in enumerate(((k_ref, ko), (v_ref, vo))):
        go(sib_copy(src.at[:, head_cols(y)], dst, mine, 0, i))


    def spread(src, dst, send, recv, pieces=(0, 2, 1)):
        for dy in (2, 1, 3, 0):
            ty = (y + dy) % 4
            for j in pieces:
                core, slot = slot_of(y, k, j)
                piece = src.at[pl.ds(j * HD, HD), head_cols(ty)]
                there = dst.at[pl.ds(pl.multiple_of(slot * HD, HD), HD)]
                if dy:
                    go(remote(piece, there, send.at[dy, j], recv.at[slot], seq_of(x, ty, core), g))
                else:
                    @pl.when(core != k)
                    def _():
                        remote(piece, there, send.at[0, j], recv.at[slot],
                               sibling, g).start()

                    @pl.when(core == k)
                    def _():
                        pltpu.make_async_copy(piece, there, recv.at[slot]).start()

    def drain(src, dst, send, recv):
        for j in range(3):
            core, slot = slot_of(y, k, j)
            piece = src.at[pl.ds(j * HD, HD), head_cols(y)]
            there = dst.at[pl.ds(pl.multiple_of(slot * HD, HD), HD)]

            @pl.when(core != k)
            def _():
                remote(piece, there, send.at[0, j], recv.at[slot],
                       sibling, g).wait_send()
        for slot in range(12):
            there = dst.at[pl.ds(slot * HD, HD)]
            pltpu.make_async_copy(there, there, recv.at[slot]).wait()

    for i in range(1, 16):
        go(remote(doc_ref, doco.at[s], d_send.at[i], d_recv.at[i], (s + i) % 16, g))
    own_doc = pltpu.make_async_copy(doc_ref, doco.at[s], d_recv.at[0])
    own_doc.start()

    def got(slot, c):
        ring(0, land.at[slot, rows(c)], slot, c, up).wait_recv()

    def relay_kv(dy):
        where = block_rows(seq_of(x, (y + 4 - dy) % 4, k))
        for i, dst in enumerate((ko, vo)):
            remote(dst.at[where], dst.at[where], y_send.at[dy, i], y_recv.at[dy, i], sibling, g).wait_recv()
            go(sib_copy(dst.at[where], dst, where, dy, i))

    def from_x(dy):
        where = block_rows(seq_of(0, (y + 4 - dy) % 4, k))

        @pl.when(x == 1)
        def _():
            for i, dst in enumerate((ko, vo)):
                x_copy(dst.at[where], dst, where, dy, i).wait_recv()
                sib_copy(dst.at[where], dst, where, 4 + dy, i).start()

    def pass_on(slot):
        for c, e in order[:3]:
            got(slot, c)
            go(ring(slot + 2, land.at[slot, rows(c)], slot + 2, c, up))
            got(slot + 1, e)
            go(ring(slot + 2, land.at[slot + 1, rows(e)], slot + 2, e, down))

    def share(c):
        got(4, c)
        go(ring(4, land.at[4, rows(c)], 5, c, up))
        go(ring(5, land.at[4, rows(c)], 6, c, down))

    pass_on(1)
    share(0)
    relay_kv(1)
    share(5)
    relay_kv(3)
    share(1)
    share(4)
    relay_kv(2)
    share(2)
    share(3)
    @pl.when(x == 0)
    def _():
        for i, (src, dst) in enumerate(((k_ref, ko), (v_ref, vo))):
            x_copy(src.at[:, head_cols(y)], dst, mine, 0, i).start()
        for dy in (1, 3, 2):
            where = block_rows(seq_of(0, (y + 4 - dy) % 4, k))
            for i, dst in enumerate((ko, vo)):
                x_copy(dst.at[where], dst, where, dy, i).start()
    spread(q_ref, qo, q_send, q_recv)

    w_copy.wait()

    def product(slot, head):
        block = land[slot]
        weights = w_ref[:, pl.ds(pl.multiple_of(head * COLS, COLS), COLS)]
        part = lax.dot_general(block, weights, NT, preferred_element_type=jnp.float32)
        acc[...] = part if slot == 0 else acc[...] + part

    far = xh * 4 + (z + 2) % 4
    turn = (1 - xh) * 4
    og_copy.wait()
    product(0, g)
    for c, e in order[:3]:
        got(1, e)
        got(2, c)
    product(1, down)
    product(2, up)
    from_x(0)
    for c, e in order[:3]:
        got(3, c)
        got(3, e)
    product(3, far)
    product(4, across)
    pass_on(5)
    from_x(1)
    for c, e in order[:3]:
        got(5, e)
        got(6, c)
    product(5, turn + (z + 3) % 4)
    product(6, turn + (z + 1) % 4)
    from_x(3)

    last = turn + (z + 2) % 4
    weights = w_ref[:, pl.ds(pl.multiple_of(last * COLS, COLS), COLS)]

    def finish(j):
        piece = pl.ds(j * HD, HD)
        part = lax.dot_general(land[7, piece], weights, NT, preferred_element_type=jnp.float32)
        grad[piece] = (acc[piece] + part).astype(jnp.bfloat16)
        spread(grad, do, o_send, o_recv, (j,))

    for c, e in order[:2]:
        got(7, c)
        got(7, e)
    finish(0)
    finish(2)
    for c in (2, 3):
        got(7, c)
    finish(1)
    from_x(2)

    for copy in local:
        copy.wait()
    own_doc.wait()
    for i in range(1, 16):
        remote(doc_ref, doco.at[(s + 16 - i) % 16], d_send.at[i], d_recv.at[i], s, g).wait_recv()
    for dy in range(4):
        where = block_rows(seq_of(x, (y + 4 - dy) % 4, 1 - k))
        for i, dst in enumerate((ko, vo)):
            sib_copy(dst.at[where], dst, where, dy, i).wait_recv()

    @pl.when(x == 0)
    def _():
        for dy in range(4):
            where = block_rows(seq_of(0, (y + 4 - dy) % 4, k))
            for i, dst in enumerate((ko, vo)):
                x_copy(dst.at[where], dst, where, dy, i).wait_send()

    @pl.when(x == 1)
    def _():
        for dy in range(4):
            where = block_rows(seq_of(0, (y + 4 - dy) % 4, 1 - k))
            for i, dst in enumerate((ko, vo)):
                copy = sib_copy(dst.at[where], dst, where, 4 + dy, i)
                copy.wait_recv()
                copy.wait_send()
    drain(q_ref, qo, q_send, q_recv)
    drain(grad, do, o_send, o_recv)
    for copy in sends:
        copy.wait_send()


def gather_call(queries, keys_in, values, out_grad, out_weight, docs):
    hbm = pl.BlockSpec(memory_space=pltpu.HBM)
    anyspace = pl.BlockSpec(memory_space=pl.ANY)
    dma = pltpu.SemaphoreType.DMA
    bf = jnp.bfloat16
    return pl.pallas_call(
        gather_kernel,
        out_shape=(
            jax.ShapeDtypeStruct((TOTAL, HD), bf),
            jax.ShapeDtypeStruct((TOTAL, HD), bf),
            jax.ShapeDtypeStruct((QLOCAL, HD), bf),
            jax.ShapeDtypeStruct((QLOCAL, HD), bf),
            jax.ShapeDtypeStruct((16, 3, HD), jnp.int32),
        ),
        in_specs=[hbm] * 6,
        out_specs=(anyspace,) * 5,
        scratch_shapes=[
            pltpu.VMEM((8, ROWS, COLS), bf),
            pltpu.VMEM((COLS, 4096), bf),
            pltpu.VMEM((ROWS, COLS), jnp.float32),
            pltpu.VMEM((ROWS, COLS), bf),
            dma((8, NCH)), dma((8, NCH)), dma((4, 2)), dma((4, 2)),
            dma((8, 2)), dma((8, 2)), dma((4, 2)), dma((4, 2)),
            dma((4, 3)), dma((12,)), dma((4, 3)), dma((12,)),
            dma((16,)), dma((16,)), dma, dma((2,)),
        ],
        compiler_params=pltpu.CompilerParams(
            collective_id=0, has_side_effects=True, vmem_limit_bytes=12 << 20
        ),
        name="spread_rows",
    )(
        *(
            pltpu.with_memory_space_constraint(a, pltpu.HBM)
            for a in (queries, keys_in, values, out_grad, out_weight, docs)
        )
    )


def attention_kernel(
    doc_v, q_ref, o_ref, k_ref, v_ref,
    dq_ref, dk_ref, dv_ref,
    p_buf, g_buf, dq_acc,
):
    s, g, x, y, k = place()
    docs = doc_v[...]
    starts = [jnp.int32(0)]
    for d in range(1, 8):
        starts.append(jnp.sum(jnp.where(docs < d, 1, 0)))

    @pl.when(x == 1)
    def _():
        dk_ref[: TOTAL // 2] = jnp.zeros((TOTAL // 2, HD), jnp.float32)
        dv_ref[: TOTAL // 2] = jnp.zeros((TOTAL // 2, HD), jnp.float32)

    factor = SCALE * LOG2E
    lane = lax.broadcasted_iota(jnp.int32, (1, QT), 1)
    sub = lax.broadcasted_iota(jnp.int32, (KT, QT), 0)
    f32 = jnp.float32

    def folded(value, reduce):
        return reduce(value.reshape(KT // 8, 8, QT), axis=0)

    @pl.loop(0, QLOCAL // QT)
    def _(t):
        diagonal = 6 * x + t
        unit = 4 * diagonal + k
        mine = pl.ds(pl.multiple_of(t * QT, QT), QT)
        q_tile = q_ref[mine, :]
        o_tile = o_ref[mine, :]
        doc_q = jnp.concatenate(
            [doc_v[u // 3, pl.ds(u % 3, 1), :] for u in (unit, unit + 2)], axis=1
        )
        start = jnp.zeros((1, QT), jnp.int32)
        for d in range(1, 8):
            start = jnp.where(doc_q == d, starts[d], start)
        k_low = jnp.min(start) // KT
        k_full = jnp.minimum((jnp.max(start) + KT - 1) // KT, diagonal)
        pos = unit * HD + lane + jnp.where(lane >= HD, HD, 0)

        def rows_of(kt):
            return pl.ds(pl.multiple_of(kt * KT, KT), KT)

        def plain(kt, top):
            scores = lax.dot_general(k_ref[rows_of(kt), :], q_tile, NT, preferred_element_type=f32)
            p_buf[kt] = scores
            return jnp.maximum(top, folded(scores, jnp.max))

        def masked(kt, top):
            scores = lax.dot_general(k_ref[rows_of(kt), :], q_tile, NT, preferred_element_type=f32)
            key = kt * KT + sub
            scores = jnp.where((key >= start) & (key <= pos), scores, NEG)
            p_buf[kt] = scores
            return jnp.maximum(top, folded(scores, jnp.max))

        top = jnp.full((8, QT), NEG, f32)
        top = lax.fori_loop(k_low, k_full, masked, top)
        top = lax.fori_loop(k_full, diagonal, plain, top)
        top = jnp.max(masked(diagonal, top), axis=0, keepdims=True)

        def weigh(kt, carry):
            total, weighted = carry
            p = jnp.exp2((p_buf[kt] - top) * factor)
            gp = lax.dot_general(v_ref[rows_of(kt), :], o_tile, NT, preferred_element_type=f32)
            p_buf[kt] = p
            g_buf[kt] = gp
            return total + folded(p, jnp.sum), weighted + folded(p * gp, jnp.sum)

        zero = jnp.zeros((8, QT), f32)
        total, weighted = lax.fori_loop(k_low, diagonal + 1, weigh, (zero, zero))
        inverse = 1.0 / jnp.sum(total, axis=0, keepdims=True)
        dot_row = jnp.sum(weighted, axis=0, keepdims=True) * inverse
        dq_acc[...] = jnp.zeros_like(dq_acc)

        def grads(kt, fresh):
            keys = rows_of(kt)
            probs = p_buf[kt] * inverse
            ds = (probs * (g_buf[kt] - dot_row)).astype(jnp.bfloat16)
            dv = lax.dot_general(
                probs.astype(jnp.bfloat16), o_tile, NN, preferred_element_type=f32
            )
            dk = lax.dot_general(ds, q_tile, NN, preferred_element_type=f32)
            if fresh:
                dv_ref[keys, :] = dv
                dk_ref[keys, :] = dk
            else:
                dv_ref[keys, :] += dv
                dk_ref[keys, :] += dk
            dq_acc[...] += lax.dot_general(k_ref[keys, :], ds, TN, preferred_element_type=f32)

        @pl.loop(k_low, diagonal)
        def _(kt):
            grads(kt, False)

        grads(diagonal, True)
        dq_ref[mine, :] = (dq_acc[...] * SCALE).T.astype(jnp.bfloat16)


def attention_call(docs, q, o, k, v):
    vm = pl.BlockSpec(memory_space=pltpu.VMEM)
    bf, f32 = jnp.bfloat16, jnp.float32
    tiles = TOTAL // KT
    return pl.pallas_call(
        attention_kernel,
        out_shape=(
            jax.ShapeDtypeStruct((QLOCAL, HD), bf),
            jax.ShapeDtypeStruct((TOTAL, HD), f32),
            jax.ShapeDtypeStruct((TOTAL, HD), f32),
        ),
        in_specs=[vm] * 5,
        out_specs=(vm, vm, vm),
        scratch_shapes=[
            pltpu.VMEM((tiles, KT, QT), f32),
            pltpu.VMEM((tiles, KT, QT), f32),
            pltpu.VMEM((HD, QT), f32),
        ],
        compiler_params=pltpu.CompilerParams(
            vmem_limit_bytes=32 << 20
        ),
        name="attention_grads",
    )(docs, q, o, k, v)


def return_kernel(
    dq_ref, dk_ref, dv_ref,
    qo, ko, vo,
    sib_buf, x_buf, pass_buf, sib_stage, stage,
    q_send, q_recv, sib_send, sib_recv, x_send, x_recv, y_send, y_recv, p_send, p_recv,
):
    s, g, x, y, k = place()
    beyond = (1 - g // 4) * 4 + g % 4
    sibling = seq_of(x, y, 1 - k)
    other = seq_of(1 - x, y, k)
    column = [(seq_of(x, (y + dy) % 4, c), g) for dy in (1, 2, 3) for c in (0, 1)]
    barrier_with(column + [(sibling, g), (other, g), (other, beyond)])
    parts = (dk_ref, dv_ref)
    first = ((0, 1), (2, 0), (2, 1), (1, 0), (1, 1), (3, 0), (3, 1), (0, 0))
    outs = (ko, vo)
    order = (2, 1, 3, 0)

    def column_of(n):
        return 1 - x if n < 4 else x

    def part(n, i, core):
        rows = block_rows(seq_of(column_of(n), (y + n) % 4, core))
        return parts[i][rows, :] * (1.0 if i else SCALE)

    def sib_copy(n, i):
        return remote(
            sib_stage.at[n, i], sib_buf.at[n, i], sib_send.at[n, i], sib_recv.at[n, i], sibling, g
        )

    def sib_start(n, i):
        sib_stage[n, i] = part(n, i, 1 - k).astype(jnp.bfloat16)
        sib_copy(n, i).start()

    def x_copy(dy, i):
        return remote(stage.at[dy, i], x_buf.at[dy, i], x_send.at[dy, i], x_recv.at[dy, i], other, g)

    def first_leg():
        return remote(stage.at[0, 1], pass_buf, p_send, p_recv, other, beyond)

    def second_leg():
        return remote(pass_buf, pass_buf, p_send, p_recv, other, g)

    def third_leg():
        return remote(pass_buf, x_buf.at[0, 1], x_send.at[0, 1], x_recv.at[0, 1], other, beyond)

    def y_copy(dy, i):
        return remote(
            stage.at[4 + dy, i], outs[i].at[:, head_cols(y)], y_send.at[dy, i], y_recv.at[dy, i],
            seq_of(x, (y + dy) % 4, k), g,
        )

    @pl.when(x == 1)
    def _():
        for dy, i in first:
            sib_start(dy, i)

    def q_piece(n):
        chip, u = 4 * x + n // 3, (n % 3) * 2 + k
        tk, j = u // 3, u % 3
        src = dq_ref.at[pl.ds(n * HD, HD)]
        dst = qo.at[pl.ds(pl.multiple_of(j * HD, HD), HD), head_cols(y)]
        return chip * 2 + tk, j, src, dst

    for n in range(12):
        to, j, src, dst = q_piece(n)

        @pl.when(to == s)
        def _():
            pltpu.make_async_copy(src, dst, q_recv.at[y, j]).start()

        @pl.when(to != s)
        def _():
            remote(src, dst, q_send.at[n], q_recv.at[y, j], to, g).start()

    for dy in order:
        for i in range(2):
            sib_start(4 + dy, i)

    def summed(n, i, extra):
        sib_copy(n, i).wait_recv()
        total = part(n, i, k) + sib_buf[n, i].astype(jnp.float32)
        if extra:
            x_copy(n - 4, i).wait_recv()
            total = total + x_buf[n - 4, i].astype(jnp.float32)
        stage[n, i] = total.astype(jnp.bfloat16)

    def own_column(extra):
        for dy in order:
            for i in range(2):
                summed(4 + dy, i, extra)
                if dy:
                    y_copy(dy, i).start()
                else:
                    pltpu.make_async_copy(
                        stage.at[4, i], outs[i].at[:, head_cols(y)], y_recv.at[0, i]
                    ).start()

    @pl.when(x == 1)
    def _():
        for dy, i in first:
            summed(dy, i, False)
            if (dy, i) == (0, 1):
                first_leg().start()
            else:
                x_copy(dy, i).start()
        second_leg().wait_recv()
        third_leg().start()
        own_column(False)

    @pl.when(x == 0)
    def _():
        first_leg().wait_recv()
        second_leg().start()
        own_column(True)
        second_leg().wait_send()

    for ty in range(4):
        for j in range(3):
            dst = qo.at[pl.ds(j * HD, HD), pl.ds(ty * HD, HD)]
            pltpu.make_async_copy(dst, dst, q_recv.at[ty, j]).wait()
    for n in range(12):
        to, j, src, dst = q_piece(n)

        @pl.when(to != s)
        def _():
            remote(src, dst, q_send.at[n], q_recv.at[y, j], to, g).wait_send()
    for dy in range(4):
        for i in range(2):
            dst = outs[i].at[:, head_cols((y + 4 - dy) % 4)]
            pltpu.make_async_copy(dst, dst, y_recv.at[dy, i]).wait()
            sib_copy(4 + dy, i).wait_send()
            if dy:
                y_copy(dy, i).wait_send()

    @pl.when(x == 1)
    def _():
        for dy in range(4):
            for i in range(2):
                sib_copy(dy, i).wait_send()
                if (dy, i) == (0, 1):
                    first_leg().wait_send()
                    third_leg().wait_send()
                else:
                    x_copy(dy, i).wait_send()


def return_call(dq, dk, dv):
    vm = pl.BlockSpec(memory_space=pltpu.VMEM)
    anyspace = pl.BlockSpec(memory_space=pl.ANY)
    dma = pltpu.SemaphoreType.DMA
    bf = jnp.bfloat16
    return pl.pallas_call(
        return_kernel,
        out_shape=(jax.ShapeDtypeStruct((ROWS, COLS), bf),) * 3,
        in_specs=[vm, vm, vm],
        out_specs=(anyspace,) * 3,
        scratch_shapes=[
            pltpu.VMEM((8, 2, ROWS, HD), bf),
            pltpu.VMEM((4, 2, ROWS, HD), bf),
            pltpu.VMEM((ROWS, HD), bf),
            pltpu.VMEM((8, 2, ROWS, HD), bf),
            pltpu.VMEM((8, 2, ROWS, HD), bf),
            dma((12,)), dma((4, 3)), dma((8, 2)), dma((8, 2)),
            dma((4, 2)), dma((4, 2)), dma((4, 2)), dma((4, 2)), dma, dma,
        ],
        compiler_params=pltpu.CompilerParams(
            collective_id=1, has_side_effects=True, vmem_limit_bytes=8 << 20
        ),
        name="return_grads",
    )(dq, dk, dv)


def store_kernel(a, b, c, ao, bo, co, sem):
    copies = [
        pltpu.make_async_copy(src, dst, sem.at[i])
        for i, (src, dst) in enumerate(((a, ao), (b, bo), (c, co)))
    ]
    for copy in copies:
        copy.start()
    for copy in copies:
        copy.wait()


def store_call(*arrays):
    vm = pl.BlockSpec(memory_space=pltpu.VMEM)
    hbm = pl.BlockSpec(memory_space=pltpu.HBM)
    return pl.pallas_call(
        store_kernel,
        out_shape=(jax.ShapeDtypeStruct((ROWS, COLS), jnp.bfloat16),) * 3,
        in_specs=[vm] * 3,
        out_specs=(hbm,) * 3,
        scratch_shapes=[pltpu.SemaphoreType.DMA((3,))],
        compiler_params=pltpu.CompilerParams(vmem_limit_bytes=4 << 20),
        name="store_grads",
    )(*arrays)


def per_device(queries, keys_in, values, out_grad, out_weight, doc_ids):
    k, v, q, o, docs = gather_call(
        queries, keys_in, values, out_grad, out_weight, doc_ids.reshape(3, HD)
    )
    dq, dk, dv = attention_call(docs, q, o, k, v)
    return store_call(*return_call(dq, dk, dv))


def solution(mesh):
    in_specs = (
        P("seq", "head"),
        P("seq", "head"),
        P("seq", "head"),
        P("seq", "head"),
        P("head", None),
        P("seq"),
    )
    out_specs = (P("seq", "head"), P("seq", "head"), P("seq", "head"))
    return jax.shard_map(
        per_device, mesh=mesh, in_specs=in_specs, out_specs=out_specs, check_vma=False
    )
```

```python
import functools

import jax
import jax.numpy as jnp
from jax import lax
from jax.experimental import pallas as pl
from jax.experimental.pallas import tpu as pltpu
from jax.sharding import PartitionSpec as P

HD = 128
ROWS = 384
COLS = 512
HEADS_LOCAL = 4
TOTAL = 6144
QT = 256
KT = 512
QLOCAL = 1536
NCH = 6
CH = ROWS // NCH
NEG = -1e30
SCALE = HD ** -0.5
LOG2E = 1.4426950408889634
MESH = pl.DeviceIdType.MESH
NT = (((1,), (1,)), ((), ()))
TN = (((0,), (0,)), ((), ()))
NN = (((1,), (0,)), ((), ()))


def place():
    s = lax.axis_index("seq")
    g = lax.axis_index("head")
    x = s // 8
    y = (s // 2) % 4
    k = s % 2
    return s, g, x, y, k


def seq_of(x, y, k):
    return (x * 4 + y) * 2 + k


def remote(src, dst, send, recv, seq, head):
    return pltpu.make_async_remote_copy(
        src_ref=src,
        dst_ref=dst,
        send_sem=send,
        recv_sem=recv,
        device_id={"seq": seq, "head": head},
        device_id_type=MESH,
    )


def barrier_with(peers):
    barrier = pltpu.get_barrier_semaphore()
    for seq, head in peers:
        pl.semaphore_signal(
            barrier, inc=1, device_id={"seq": seq, "head": head}, device_id_type=MESH
        )
    pl.semaphore_wait(barrier, len(peers))


def block_rows(s):
    return pl.ds(pl.multiple_of(s * ROWS, 128), ROWS)


def head_cols(y):
    return pl.ds(pl.multiple_of(y * HD, HD), HD)


def slot_of(y, k, j):
    u = 3 * k + j
    return u % 2, 3 * y + u // 2


def gather_kernel(
    q_ref, k_ref, v_ref, og_hbm, w_hbm, doc_ref,
    ko, vo, qo, do, doco,
    land, w_ref, acc, grad,
    g_send, g_recv, y_send, y_recv, sib_send, sib_recv, x_send, x_recv,
    q_send, q_recv, o_send, o_recv, d_send, d_recv, w_sem, l_sem,
):
    s, g, x, y, k = place()
    xh, z = g // 4, g % 4
    up = xh * 4 + (z + 1) % 4
    down = xh * 4 + (z + 3) % 4
    across = (1 - xh) * 4 + z
    sibling = seq_of(x, y, 1 - k)
    other = seq_of(1 - x, y, k)

    og_copy = pltpu.make_async_copy(og_hbm, land.at[0], g_recv.at[0, 0])
    og_copy.start()
    w_copy = pltpu.make_async_copy(w_hbm, w_ref, w_sem)
    w_copy.start()
    barrier_with(
        [((s + i) % 16, g) for i in range(1, 16)] + [(s, up), (s, down), (s, across)]
    )

    sends = []

    def go(copy):
        copy.start()
        sends.append(copy)

    def rows(c):
        return pl.ds(c * CH, CH)

    order = ((0, 5), (1, 4), (2, 3), (3, 2), (4, 1), (5, 0))

    def ring(n, src, slot, c, head):
        return remote(src, land.at[slot, rows(c)], g_send.at[n, c], g_recv.at[slot, c], s, head)

    for (up_c, down_c), across_c in zip(order, (0, 5, 1, 4, 2, 3)):
        go(ring(0, og_hbm.at[rows(up_c)], 1, up_c, up))
        go(ring(1, og_hbm.at[rows(down_c)], 2, down_c, down))
        go(ring(2, og_hbm.at[rows(across_c)], 4, across_c, across))

    mine = block_rows(s)
    local = []
    for i, (src, dst) in enumerate(((k_ref, ko), (v_ref, vo))):
        copy = pltpu.make_async_copy(src.at[:, head_cols(y)], dst.at[mine], l_sem.at[i])
        copy.start()
        local.append(copy)
    for dy in (2, 1, 3):
        ty = (y + dy) % 4
        for i, (src, dst) in enumerate(((k_ref, ko), (v_ref, vo))):
            go(remote(src.at[:, head_cols(ty)], dst.at[mine], y_send.at[dy, i],
                      y_recv.at[dy, i], seq_of(x, ty, k), g))

    def x_copy(src, dst, where, dy, i):
        return remote(src, dst.at[where], x_send.at[dy, i], x_recv.at[dy, i], other, g)

    def sib_copy(src, dst, where, n, i):
        return remote(src, dst.at[where], sib_send.at[n, i], sib_recv.at[n, i], sibling, g)

    for i, (src, dst) in enumerate(((k_ref, ko), (v_ref, vo))):
        go(sib_copy(src.at[:, head_cols(y)], dst, mine, 0, i))


    def spread(src, dst, send, recv, pieces=(0, 2, 1)):
        for dy in (2, 1, 3, 0):
            ty = (y + dy) % 4
            for j in pieces:
                core, slot = slot_of(y, k, j)
                piece = src.at[pl.ds(j * HD, HD), head_cols(ty)]
                there = dst.at[pl.ds(pl.multiple_of(slot * HD, HD), HD)]
                if dy:
                    go(remote(piece, there, send.at[dy, j], recv.at[slot], seq_of(x, ty, core), g))
                else:
                    @pl.when(core != k)
                    def _():
                        remote(piece, there, send.at[0, j], recv.at[slot],
                               sibling, g).start()

                    @pl.when(core == k)
                    def _():
                        pltpu.make_async_copy(piece, there, recv.at[slot]).start()

    def drain(src, dst, send, recv):
        for j in range(3):
            core, slot = slot_of(y, k, j)
            piece = src.at[pl.ds(j * HD, HD), head_cols(y)]
            there = dst.at[pl.ds(pl.multiple_of(slot * HD, HD), HD)]

            @pl.when(core != k)
            def _():
                remote(piece, there, send.at[0, j], recv.at[slot],
                       sibling, g).wait_send()
        for slot in range(12):
            there = dst.at[pl.ds(slot * HD, HD)]
            pltpu.make_async_copy(there, there, recv.at[slot]).wait()

    for i in range(1, 16):
        go(remote(doc_ref, doco.at[s], d_send.at[i], d_recv.at[i], (s + i) % 16, g))
    own_doc = pltpu.make_async_copy(doc_ref, doco.at[s], d_recv.at[0])
    own_doc.start()

    def got(slot, c):
        ring(0, land.at[slot, rows(c)], slot, c, up).wait_recv()

    def relay_kv(dy):
        where = block_rows(seq_of(x, (y + 4 - dy) % 4, k))
        for i, dst in enumerate((ko, vo)):
            remote(dst.at[where], dst.at[where], y_send.at[dy, i], y_recv.at[dy, i], sibling, g).wait_recv()
            go(sib_copy(dst.at[where], dst, where, dy, i))

    def from_x(dy):
        where = block_rows(seq_of(0, (y + 4 - dy) % 4, k))

        @pl.when(x == 1)
        def _():
            for i, dst in enumerate((ko, vo)):
                x_copy(dst.at[where], dst, where, dy, i).wait_recv()
                sib_copy(dst.at[where], dst, where, 4 + dy, i).start()

    def pass_on(slot):
        for c, e in order[:3]:
            got(slot, c)
            go(ring(slot + 2, land.at[slot, rows(c)], slot + 2, c, up))
            got(slot + 1, e)
            go(ring(slot + 2, land.at[slot + 1, rows(e)], slot + 2, e, down))

    def share(c):
        got(4, c)
        go(ring(4, land.at[4, rows(c)], 5, c, up))
        go(ring(5, land.at[4, rows(c)], 6, c, down))

    pass_on(1)
    share(0)
    relay_kv(1)
    share(5)
    relay_kv(3)
    share(1)
    share(4)
    relay_kv(2)
    share(2)
    share(3)
    @pl.when(x == 0)
    def _():
        for i, (src, dst) in enumerate(((k_ref, ko), (v_ref, vo))):
            x_copy(src.at[:, head_cols(y)], dst, mine, 0, i).start()
        for dy in (1, 3, 2):
            where = block_rows(seq_of(0, (y + 4 - dy) % 4, k))
            for i, dst in enumerate((ko, vo)):
                x_copy(dst.at[where], dst, where, dy, i).start()
    spread(q_ref, qo, q_send, q_recv)

    w_copy.wait()

    def product(slot, head):
        block = land[slot]
        weights = w_ref[:, pl.ds(pl.multiple_of(head * COLS, COLS), COLS)]
        part = lax.dot_general(block, weights, NT, preferred_element_type=jnp.float32)
        acc[...] = part if slot == 0 else acc[...] + part

    far = xh * 4 + (z + 2) % 4
    turn = (1 - xh) * 4
    og_copy.wait()
    product(0, g)
    for c, e in order[:3]:
        got(1, e)
        got(2, c)
    product(1, down)
    product(2, up)
    from_x(0)
    for c, e in order[:3]:
        got(3, c)
        got(3, e)
    product(3, far)
    product(4, across)
    pass_on(5)
    from_x(1)
    for c, e in order[:3]:
        got(5, e)
        got(6, c)
    product(5, turn + (z + 3) % 4)
    product(6, turn + (z + 1) % 4)
    from_x(3)

    last = turn + (z + 2) % 4
    weights = w_ref[:, pl.ds(pl.multiple_of(last * COLS, COLS), COLS)]

    def finish(j):
        piece = pl.ds(j * HD, HD)
        part = lax.dot_general(land[7, piece], weights, NT, preferred_element_type=jnp.float32)
        grad[piece] = (acc[piece] + part).astype(jnp.bfloat16)
        spread(grad, do, o_send, o_recv, (j,))

    for c, e in order[:2]:
        got(7, c)
        got(7, e)
    finish(0)
    finish(2)
    for c in (2, 3):
        got(7, c)
    finish(1)
    from_x(2)

    for copy in local:
        copy.wait()
    own_doc.wait()
    for i in range(1, 16):
        remote(doc_ref, doco.at[(s + 16 - i) % 16], d_send.at[i], d_recv.at[i], s, g).wait_recv()
    for dy in range(4):
        where = block_rows(seq_of(x, (y + 4 - dy) % 4, 1 - k))
        for i, dst in enumerate((ko, vo)):
            sib_copy(dst.at[where], dst, where, dy, i).wait_recv()

    @pl.when(x == 0)
    def _():
        for dy in range(4):
            where = block_rows(seq_of(0, (y + 4 - dy) % 4, k))
            for i, dst in enumerate((ko, vo)):
                x_copy(dst.at[where], dst, where, dy, i).wait_send()

    @pl.when(x == 1)
    def _():
        for dy in range(4):
            where = block_rows(seq_of(0, (y + 4 - dy) % 4, 1 - k))
            for i, dst in enumerate((ko, vo)):
                copy = sib_copy(dst.at[where], dst, where, 4 + dy, i)
                copy.wait_recv()
                copy.wait_send()
    drain(q_ref, qo, q_send, q_recv)
    drain(grad, do, o_send, o_recv)
    for copy in sends:
        copy.wait_send()


def gather_call(queries, keys_in, values, out_grad, out_weight, docs):
    hbm = pl.BlockSpec(memory_space=pltpu.HBM)
    anyspace = pl.BlockSpec(memory_space=pl.ANY)
    dma = pltpu.SemaphoreType.DMA
    bf = jnp.bfloat16
    return pl.pallas_call(
        gather_kernel,
        out_shape=(
            jax.ShapeDtypeStruct((TOTAL, HD), bf),
            jax.ShapeDtypeStruct((TOTAL, HD), bf),
            jax.ShapeDtypeStruct((QLOCAL, HD), bf),
            jax.ShapeDtypeStruct((QLOCAL, HD), bf),
            jax.ShapeDtypeStruct((16, 3, HD), jnp.int32),
        ),
        in_specs=[hbm] * 6,
        out_specs=(anyspace,) * 5,
        scratch_shapes=[
            pltpu.VMEM((8, ROWS, COLS), bf),
            pltpu.VMEM((COLS, 4096), bf),
            pltpu.VMEM((ROWS, COLS), jnp.float32),
            pltpu.VMEM((ROWS, COLS), bf),
            dma((8, NCH)), dma((8, NCH)), dma((4, 2)), dma((4, 2)),
            dma((8, 2)), dma((8, 2)), dma((4, 2)), dma((4, 2)),
            dma((4, 3)), dma((12,)), dma((4, 3)), dma((12,)),
            dma((16,)), dma((16,)), dma, dma((2,)),
        ],
        compiler_params=pltpu.CompilerParams(
            collective_id=0, has_side_effects=True, vmem_limit_bytes=12 << 20
        ),
        name="spread_rows",
    )(
        *(
            pltpu.with_memory_space_constraint(a, pltpu.HBM)
            for a in (queries, keys_in, values, out_grad, out_weight, docs)
        )
    )


def attention_kernel(
    doc_v, q_ref, o_ref, k_ref, v_ref,
    dq_ref, dk_ref, dv_ref,
    p_buf, g_buf, dq_acc,
):
    s, g, x, y, k = place()
    docs = doc_v[...]
    starts = [jnp.int32(0)]
    for d in range(1, 8):
        starts.append(jnp.sum(jnp.where(docs < d, 1, 0)))

    @pl.when(x == 1)
    def _():
        dk_ref[: TOTAL // 2] = jnp.zeros((TOTAL // 2, HD), jnp.float32)
        dv_ref[: TOTAL // 2] = jnp.zeros((TOTAL // 2, HD), jnp.float32)

    factor = SCALE * LOG2E
    lane = lax.broadcasted_iota(jnp.int32, (1, QT), 1)
    sub = lax.broadcasted_iota(jnp.int32, (KT, QT), 0)
    f32 = jnp.float32

    def folded(value, reduce):
        return reduce(value.reshape(KT // 8, 8, QT), axis=0)

    @pl.loop(0, QLOCAL // QT)
    def _(t):
        diagonal = 6 * x + t
        unit = 4 * diagonal + k
        mine = pl.ds(pl.multiple_of(t * QT, QT), QT)
        q_tile = q_ref[mine, :]
        o_tile = o_ref[mine, :]
        doc_q = jnp.concatenate(
            [doc_v[u // 3, pl.ds(u % 3, 1), :] for u in (unit, unit + 2)], axis=1
        )
        start = jnp.zeros((1, QT), jnp.int32)
        for d in range(1, 8):
            start = jnp.where(doc_q == d, starts[d], start)
        k_low = jnp.min(start) // KT
        k_full = jnp.minimum((jnp.max(start) + KT - 1) // KT, diagonal)
        pos = unit * HD + lane + jnp.where(lane >= HD, HD, 0)

        def rows_of(kt):
            return pl.ds(pl.multiple_of(kt * KT, KT), KT)

        def plain(kt, top):
            scores = lax.dot_general(k_ref[rows_of(kt), :], q_tile, NT, preferred_element_type=f32)
            p_buf[kt] = scores
            return jnp.maximum(top, folded(scores, jnp.max))

        def masked(kt, top):
            scores = lax.dot_general(k_ref[rows_of(kt), :], q_tile, NT, preferred_element_type=f32)
            key = kt * KT + sub
            scores = jnp.where((key >= start) & (key <= pos), scores, NEG)
            p_buf[kt] = scores
            return jnp.maximum(top, folded(scores, jnp.max))

        top = jnp.full((8, QT), NEG, f32)
        top = lax.fori_loop(k_low, k_full, masked, top)
        top = lax.fori_loop(k_full, diagonal, plain, top)
        top = jnp.max(masked(diagonal, top), axis=0, keepdims=True)

        def weigh(kt, carry):
            total, weighted = carry
            p = jnp.exp2((p_buf[kt] - top) * factor)
            gp = lax.dot_general(v_ref[rows_of(kt), :], o_tile, NT, preferred_element_type=f32)
            p_buf[kt] = p
            g_buf[kt] = gp
            return total + folded(p, jnp.sum), weighted + folded(p * gp, jnp.sum)

        zero = jnp.zeros((8, QT), f32)
        total, weighted = lax.fori_loop(k_low, diagonal + 1, weigh, (zero, zero))
        inverse = 1.0 / jnp.sum(total, axis=0, keepdims=True)
        dot_row = jnp.sum(weighted, axis=0, keepdims=True) * inverse
        dq_acc[...] = jnp.zeros_like(dq_acc)

        def grads(kt, fresh):
            keys = rows_of(kt)
            probs = p_buf[kt] * inverse
            ds = (probs * (g_buf[kt] - dot_row)).astype(jnp.bfloat16)
            dv = lax.dot_general(
                probs.astype(jnp.bfloat16), o_tile, NN, preferred_element_type=f32
            )
            dk = lax.dot_general(ds, q_tile, NN, preferred_element_type=f32)
            if fresh:
                dv_ref[keys, :] = dv
                dk_ref[keys, :] = dk
            else:
                dv_ref[keys, :] += dv
                dk_ref[keys, :] += dk
            dq_acc[...] += lax.dot_general(k_ref[keys, :], ds, TN, preferred_element_type=f32)

        @pl.loop(k_low, diagonal)
        def _(kt):
            grads(kt, False)

        grads(diagonal, True)
        dq_ref[mine, :] = (dq_acc[...] * SCALE).T.astype(jnp.bfloat16)


def attention_call(docs, q, o, k, v):
    vm = pl.BlockSpec(memory_space=pltpu.VMEM)
    bf, f32 = jnp.bfloat16, jnp.float32
    tiles = TOTAL // KT
    return pl.pallas_call(
        attention_kernel,
        out_shape=(
            jax.ShapeDtypeStruct((QLOCAL, HD), bf),
            jax.ShapeDtypeStruct((TOTAL, HD), f32),
            jax.ShapeDtypeStruct((TOTAL, HD), f32),
        ),
        in_specs=[vm] * 5,
        out_specs=(vm, vm, vm),
        scratch_shapes=[
            pltpu.VMEM((tiles, KT, QT), f32),
            pltpu.VMEM((tiles, KT, QT), f32),
            pltpu.VMEM((HD, QT), f32),
        ],
        compiler_params=pltpu.CompilerParams(
            vmem_limit_bytes=32 << 20
        ),
        name="attention_grads",
    )(docs, q, o, k, v)


def return_kernel(
    dq_ref, dk_ref, dv_ref,
    qo, ko, vo,
    sib_buf, x_buf, pass_buf, sib_stage, stage,
    q_send, q_recv, sib_send, sib_recv, x_send, x_recv, y_send, y_recv, p_send, p_recv,
):
    s, g, x, y, k = place()
    beyond = (1 - g // 4) * 4 + g % 4
    sibling = seq_of(x, y, 1 - k)
    other = seq_of(1 - x, y, k)
    column = [(seq_of(x, (y + dy) % 4, c), g) for dy in (1, 2, 3) for c in (0, 1)]
    barrier_with(column + [(sibling, g), (other, g), (other, beyond)])
    parts = (dk_ref, dv_ref)
    first = ((0, 1), (2, 0), (2, 1), (1, 0), (1, 1), (3, 0), (3, 1), (0, 0))
    outs = (ko, vo)
    order = (2, 1, 3, 0)

    def column_of(n):
        return 1 - x if n < 4 else x

    def part(n, i, core):
        rows = block_rows(seq_of(column_of(n), (y + n) % 4, core))
        return parts[i][rows, :] * (1.0 if i else SCALE)

    def sib_copy(n, i):
        return remote(
            sib_stage.at[n, i], sib_buf.at[n, i], sib_send.at[n, i], sib_recv.at[n, i], sibling, g
        )

    def sib_start(n, i):
        sib_stage[n, i] = part(n, i, 1 - k).astype(jnp.bfloat16)
        sib_copy(n, i).start()

    def x_copy(dy, i):
        return remote(stage.at[dy, i], x_buf.at[dy, i], x_send.at[dy, i], x_recv.at[dy, i], other, g)

    def first_leg():
        return remote(stage.at[0, 1], pass_buf, p_send, p_recv, other, beyond)

    def second_leg():
        return remote(pass_buf, pass_buf, p_send, p_recv, other, g)

    def third_leg():
        return remote(pass_buf, x_buf.at[0, 1], x_send.at[0, 1], x_recv.at[0, 1], other, beyond)

    def y_copy(dy, i):
        return remote(
            stage.at[4 + dy, i], outs[i].at[:, head_cols(y)], y_send.at[dy, i], y_recv.at[dy, i],
            seq_of(x, (y + dy) % 4, k), g,
        )

    @pl.when(x == 1)
    def _():
        for dy, i in first:
            sib_start(dy, i)

    def q_piece(n):
        chip, u = 4 * x + n // 3, (n % 3) * 2 + k
        tk, j = u // 3, u % 3
        src = dq_ref.at[pl.ds(n * HD, HD)]
        dst = qo.at[pl.ds(pl.multiple_of(j * HD, HD), HD), head_cols(y)]
        return chip * 2 + tk, j, src, dst

    for n in range(12):
        to, j, src, dst = q_piece(n)

        @pl.when(to == s)
        def _():
            pltpu.make_async_copy(src, dst, q_recv.at[y, j]).start()

        @pl.when(to != s)
        def _():
            remote(src, dst, q_send.at[n], q_recv.at[y, j], to, g).start()

    def own_to_sibling():
        for dy in order:
            for i in range(2):
                sib_start(4 + dy, i)

    @pl.when(x == 0)
    def _():
        own_to_sibling()

    def summed(n, i, extra):
        sib_copy(n, i).wait_recv()
        total = part(n, i, k) + sib_buf[n, i].astype(jnp.float32)
        if extra:
            x_copy(n - 4, i).wait_recv()
            total = total + x_buf[n - 4, i].astype(jnp.float32)
        stage[n, i] = total.astype(jnp.bfloat16)

    def own_column(extra):
        for dy in order:
            for i in range(2):
                summed(4 + dy, i, extra)
                if dy:
                    y_copy(dy, i).start()
                else:
                    pltpu.make_async_copy(
                        stage.at[4, i], outs[i].at[:, head_cols(y)], y_recv.at[0, i]
                    ).start()

    @pl.when(x == 1)
    def _():
        for dy, i in first:
            summed(dy, i, False)
            if (dy, i) == (0, 1):
                first_leg().start()
            else:
                x_copy(dy, i).start()
        own_to_sibling()
        second_leg().wait_recv()
        third_leg().start()
        own_column(False)

    @pl.when(x == 0)
    def _():
        first_leg().wait_recv()
        second_leg().start()
        own_column(True)
        second_leg().wait_send()

    for ty in range(4):
        for j in range(3):
            dst = qo.at[pl.ds(j * HD, HD), pl.ds(ty * HD, HD)]
            pltpu.make_async_copy(dst, dst, q_recv.at[ty, j]).wait()
    for n in range(12):
        to, j, src, dst = q_piece(n)

        @pl.when(to != s)
        def _():
            remote(src, dst, q_send.at[n], q_recv.at[y, j], to, g).wait_send()
    for dy in range(4):
        for i in range(2):
            dst = outs[i].at[:, head_cols((y + 4 - dy) % 4)]
            pltpu.make_async_copy(dst, dst, y_recv.at[dy, i]).wait()
            sib_copy(4 + dy, i).wait_send()
            if dy:
                y_copy(dy, i).wait_send()

    @pl.when(x == 1)
    def _():
        for dy in range(4):
            for i in range(2):
                sib_copy(dy, i).wait_send()
                if (dy, i) == (0, 1):
                    first_leg().wait_send()
                    third_leg().wait_send()
                else:
                    x_copy(dy, i).wait_send()


def return_call(dq, dk, dv):
    vm = pl.BlockSpec(memory_space=pltpu.VMEM)
    anyspace = pl.BlockSpec(memory_space=pl.ANY)
    dma = pltpu.SemaphoreType.DMA
    bf = jnp.bfloat16
    return pl.pallas_call(
        return_kernel,
        out_shape=(jax.ShapeDtypeStruct((ROWS, COLS), bf),) * 3,
        in_specs=[vm, vm, vm],
        out_specs=(anyspace,) * 3,
        scratch_shapes=[
            pltpu.VMEM((8, 2, ROWS, HD), bf),
            pltpu.VMEM((4, 2, ROWS, HD), bf),
            pltpu.VMEM((ROWS, HD), bf),
            pltpu.VMEM((8, 2, ROWS, HD), bf),
            pltpu.VMEM((8, 2, ROWS, HD), bf),
            dma((12,)), dma((4, 3)), dma((8, 2)), dma((8, 2)),
            dma((4, 2)), dma((4, 2)), dma((4, 2)), dma((4, 2)), dma, dma,
        ],
        compiler_params=pltpu.CompilerParams(
            collective_id=1, has_side_effects=True, vmem_limit_bytes=8 << 20
        ),
        name="return_grads",
    )(dq, dk, dv)


def store_kernel(a, b, c, ao, bo, co, sem):
    copies = [
        pltpu.make_async_copy(src, dst, sem.at[i])
        for i, (src, dst) in enumerate(((a, ao), (b, bo), (c, co)))
    ]
    for copy in copies:
        copy.start()
    for copy in copies:
        copy.wait()


def store_call(*arrays):
    vm = pl.BlockSpec(memory_space=pltpu.VMEM)
    hbm = pl.BlockSpec(memory_space=pltpu.HBM)
    return pl.pallas_call(
        store_kernel,
        out_shape=(jax.ShapeDtypeStruct((ROWS, COLS), jnp.bfloat16),) * 3,
        in_specs=[vm] * 3,
        out_specs=(hbm,) * 3,
        scratch_shapes=[pltpu.SemaphoreType.DMA((3,))],
        compiler_params=pltpu.CompilerParams(vmem_limit_bytes=4 << 20),
        name="store_grads",
    )(*arrays)


def per_device(queries, keys_in, values, out_grad, out_weight, doc_ids):
    k, v, q, o, docs = gather_call(
        queries, keys_in, values, out_grad, out_weight, doc_ids.reshape(3, HD)
    )
    dq, dk, dv = attention_call(docs, q, o, k, v)
    return store_call(*return_call(dq, dk, dv))


def solution(mesh):
    in_specs = (
        P("seq", "head"),
        P("seq", "head"),
        P("seq", "head"),
        P("seq", "head"),
        P("head", None),
        P("seq"),
    )
    out_specs = (P("seq", "head"), P("seq", "head"), P("seq", "head"))
    return jax.shard_map(
        per_device, mesh=mesh, in_specs=in_specs, out_specs=out_specs, check_vma=False
    )
```
